32 devices in a mesh: dp: 8 (over z, x), tensor: 4 (over y, core).
Axes of the slice: x: 2, y: 2, z: 4, core: 2. Of those that a mesh axis runs over, the one named last changes fastest.
Arguments:
- tokens: bfloat16 [32768, 768], P(('dp', 'tensor')), may hold values from -6 to 6
- cotangent: bfloat16 [32768, 768], P(('dp', 'tensor')), may hold values from -26 to 26
- seq_group: int32 [16], P('dp'), may hold values from 0 to 1
- block_slot: int32 [13830], replicated, may hold values from 0 to 20751, as said below
- master: float32 [4, 20752, 128], P('tensor', 'dp'), may hold values from -3 to 3
- first_moment: float32 [4, 20752, 128], P('tensor', 'dp'), may hold values from -1 to 1
- second_moment: float32 [4, 20752, 128], P('tensor', 'dp'), may hold values from 0 to 1, as said below
Outputs:
- output: bfloat16 [32768, 768], P(('dp', 'tensor'))
- input_grad: float32 [32768, 768], P(('dp', 'tensor'))
- group_norms: float32 [16], P('dp')
- new_master: float32 [4, 20752, 128], P('tensor', 'dp')
- new_first: float32 [4, 20752, 128], P('tensor', 'dp')
- new_second: float32 [4, 20752, 128], P('tensor', 'dp')
The draws below stay inside these ranges and needn't reach their ends.
Inputs may be any that keep to these rules, and one draw needn't show every extreme that they name: `block_slot`: all entries differ; slot s belongs to the owner with dp index s // 2594; one owner holds 2594 blocks. `seq_group`: group ids count within one dp index: sequences of different dp indices never share a group. `second_moment`: Positive.
All inputs are finite; a program needn't handle non-finite values.
Results may differ from the reference program's by a relative error of at most 0.012.
Values may be sent and summed in bfloat16 or wider, within the bound.
No kernel may reach another device: no remote copies, remote signals or barrier semaphores. Data moves between devices by JAX's collectives and lax.ppermute only.
A program may use at most 256 MiB of HBM per device.

```python
import math
import jax
import jax.numpy as jnp
from jax import lax

D = 768
HEADS = 12
HD = 64
ROT = 16
FF = 3072
SEQ_LEN = 2048
SEQ_DEV = 2
BLOCK_W = 128
SEQS = 16
TOKENS = 32768
NB = 13830
CAP = 2594
N_DP = 8
N_TENSOR = 4


def slot_plan(key):
    base_key = jax.random.fold_in(key, 17)
    key_owner, key_order, key_rest = jax.random.split(base_key, 3)
    busiest = jax.random.randint(key_owner, (), 0, N_DP)
    order = jax.random.permutation(key_order, NB)
    others = jax.random.permutation(key_rest, (N_DP - 1) * CAP)[:NB - CAP]
    other_owner = others // CAP
    other_owner = other_owner + (other_owner >= busiest).astype(jnp.int32)
    other_slot = other_owner * CAP + others % CAP
    chosen = jnp.concatenate([busiest * CAP + jnp.arange(CAP, dtype=jnp.int32), other_slot.astype(jnp.int32)])
    return jnp.zeros((NB,), jnp.int32).at[order].set(chosen)


def slot_kinds(key):
    slots = slot_plan(key)
    slot_block = jnp.zeros((N_DP * CAP,), jnp.int32).at[slots].set(jnp.arange(NB, dtype=jnp.int32))
    position = slot_block[:, None] * BLOCK_W + jnp.arange(BLOCK_W, dtype=jnp.int32)[None, :]
    heads_local = HEADS // N_TENSOR
    end_qkv = D * 3 * heads_local * HD
    end_out = end_qkv + heads_local * HD * D
    end_up = end_out + D * (FF // N_TENSOR)
    end_down = end_up + FF // N_TENSOR * D
    norm_index = jnp.maximum(position - end_down, 0) // (D // N_TENSOR)
    return jnp.where(position < end_qkv, 0, jnp.where(position < end_out, 1, jnp.where(position < end_up, 2, jnp.where(position < end_down, 3, 4 + norm_index % 2))))


def grad_sizes():
    typical = jnp.array([1.0, 0.05, 0.3, 0.65, 1.0, 1.0], jnp.float32)
    energy = 3.0 * D * D + 0.0025 * D * D + 0.09 * D * FF + 0.42 * FF * D + 4.0 * D
    return typical * (0.75 * SEQS / energy) ** 0.5


def draw_block_slot(key, part):
    return slot_plan(key)


def draw_master(key, part):
    kinds = slot_kinds(key)
    spread = jnp.array([D ** (-0.5), (SEQ_LEN / (5.0 * D)) ** 0.5, D ** (-0.5), FF ** (-0.5), 0.1, 0.1], jnp.float32)
    centre = jnp.array([0.0, 0.0, 0.0, 0.0, 1.0, 0.0], jnp.float32)
    noise = jax.random.truncated_normal(jax.random.fold_in(key, 31), -4.0, 4.0, (N_TENSOR, N_DP * CAP, BLOCK_W))
    return centre[kinds][None] + spread[kinds][None] * noise


def draw_first_moment(key, part):
    kinds = slot_kinds(key)
    noise = jax.random.truncated_normal(jax.random.fold_in(key, 37), -4.0, 4.0, (N_TENSOR, N_DP * CAP, BLOCK_W))
    return grad_sizes()[kinds][None] * noise


def draw_second_moment(key, part):
    kinds = slot_kinds(key)
    sizes_sq = grad_sizes()[kinds][None] ** 2
    factor = jnp.exp(jax.random.uniform(jax.random.fold_in(key, 41), (N_TENSOR, N_DP * CAP, BLOCK_W), minval=math.log(0.5), maxval=math.log(2.0)))
    return sizes_sq * (0.4 / 0.6) * 2.0 * factor


def draw_cotangent(key, part):
    base_key = jax.random.fold_in(key, 29)
    key_cols, key_rows, key_main = jax.random.split(base_key, 3)
    col_scale = jnp.exp(jax.random.uniform(key_cols, (1, D), minval=math.log(0.35), maxval=math.log(3.5)))
    row_scale = jnp.exp(jax.random.uniform(key_rows, (TOKENS, 1), minval=math.log(0.6), maxval=math.log(1.7)))
    base_value = jax.random.truncated_normal(key_main, -4.0, 4.0, (TOKENS, D))
    return (base_value * col_scale * row_scale).astype(jnp.bfloat16)


def place_ends(drawn, key, low, high):
    index_at = [jax.random.randint(jax.random.fold_in(key, axis), (), 0, length) for axis, length in enumerate(drawn.shape)]
    widest = drawn.shape.index(max(drawn.shape))
    next_to = index_at[:widest] + [(index_at[widest] + 1) % drawn.shape[widest]] + index_at[widest + 1:]
    return drawn.at[tuple(index_at)].set(low).at[tuple(next_to)].set(high)


def block_levels(stream_key, shape, cuts, least, top_value):
    gain, own = 1.0, jax.random.fold_in(stream_key, 6)
    for dim, shards_of in cuts:
        draws = jnp.exp(jax.random.uniform(jax.random.fold_in(own, dim), (shards_of,), jnp.float32, least / len(cuts), top_value / len(cuts)))
        gain = gain * jnp.repeat(draws, shape[dim] // shards_of).reshape([-1 if axis == dim else 1 for axis in range(len(shape))])
    return gain


def normal_values(stream_key, extent, width, bound, cuts=(), held_as=jnp.bfloat16):
    entries = jax.random.normal(stream_key, extent, jnp.float32) * width
    if len(cuts) > 0:
        entries = block_levels(stream_key, extent, cuts, -0.22, 0.18) * entries
    return jnp.clip(entries, min=-bound, max=bound).astype(held_as)


def setup_inputs(seed: int = 0) -> dict:
    keys = jax.random.split(jax.random.key(seed), 8)
    return {
        "tokens": normal_values(keys[0], (TOKENS, D), 1.0, 6.0, ((0, 32),)),
        "cotangent": draw_cotangent(jax.random.fold_in(keys[7], 71), 0),
        "seq_group": place_ends(jax.random.randint(keys[2], (SEQS,), 0, SEQ_DEV), jax.random.fold_in(keys[2], 1), 0, SEQ_DEV - 1).astype(jnp.int32),
        "block_slot": draw_block_slot(jax.random.fold_in(keys[7], 71), 0),
        "master": draw_master(jax.random.fold_in(keys[7], 71), 0),
        "first_moment": draw_first_moment(jax.random.fold_in(keys[7], 71), 0),
        "second_moment": draw_second_moment(jax.random.fold_in(keys[7], 71), 0),
    }


eps_norm = 1e-05
eps_adam = 1e-08
beta_one = 0.5
beta_two = 0.6

@jax.custom_vjp
def low(v):
    return lax.optimization_barrier(v.astype(jnp.bfloat16)).astype(jnp.float32)

@jax.custom_vjp
def low_back(v):
    return v

def low_keep(v):
    return (low(v), None)

def low_pass(kept, grad):
    return (grad,)

def back_keep(v):
    return (v, None)

def back_low(kept, grad):
    return (low(grad),)
low.defvjp(low_keep, low_pass)
low_back.defvjp(back_keep, back_low)

def rotary_tables(length, rot_dims):
    half_rot = rot_dims // 2
    frequency = 10000.0 ** (-2.0 * jnp.arange(half_rot, dtype=jnp.float32) / rot_dims)
    angles = jnp.arange(length, dtype=jnp.float32)[:, None] * frequency[None, :]
    return (jnp.cos(angles), jnp.sin(angles))

def rotate(features, cosine, sine_table, rot_dims):
    half_rot = rot_dims // 2
    first_half = features[..., :half_rot]
    second_half = features[..., half_rot:rot_dims]
    cos_cols = cosine[:, None, :]
    sin_cols = sine_table[:, None, :]
    return jnp.concatenate([first_half * cos_cols - second_half * sin_cols, second_half * cos_cols + first_half * sin_cols, features[..., rot_dims:]], axis=-1)

def layer_norm(rows_in):
    row_mean = lax.optimization_barrier(jnp.mean(rows_in, axis=-1, keepdims=True))
    centred = rows_in - row_mean
    inverse = lax.rsqrt(lax.optimization_barrier(jnp.mean(centred * centred, axis=-1, keepdims=True)) + eps_norm)
    return (centred * inverse, inverse)

def unpack(flat_params, d_model, heads_local, ff_local, width_local):
    inner_width = heads_local * HD
    end_qkv = d_model * 3 * inner_width
    end_out = end_qkv + inner_width * d_model
    end_up = end_out + d_model * ff_local
    end_down = end_up + ff_local * d_model
    return (flat_params[:end_qkv].reshape(d_model, 3 * inner_width), flat_params[end_qkv:end_out].reshape(inner_width, d_model), flat_params[end_out:end_up].reshape(d_model, ff_local), flat_params[end_up:end_down].reshape(ff_local, d_model), flat_params[end_down:].reshape(4, width_local))

def step_rates(position, d_model, heads_local, head_dim, ff_local, seq_len, ff_all):
    end_qkv = d_model * 3 * heads_local * head_dim
    end_out = end_qkv + heads_local * head_dim * d_model
    end_up = end_out + d_model * ff_local
    end_down = end_up + ff_local * d_model
    matrix_rate = d_model ** (-0.5)
    learn_rate = jnp.where(position < end_qkv, matrix_rate, jnp.where(position < end_out, (seq_len / (5.0 * d_model)) ** 0.5, jnp.where(position < end_up, matrix_rate, jnp.where(position < end_down, ff_all ** (-0.5), 0.1))))
    weight_decay = jnp.where(position < end_down, 0.1, 0.0)
    return (learn_rate.astype(jnp.float32), weight_decay.astype(jnp.float32))

def adam_update(weight, moment_one, moment_two, gradient, learn_rate, weight_decay):
    new_one = beta_one * moment_one + (1.0 - beta_one) * gradient
    new_two = beta_two * moment_two + (1.0 - beta_two) * gradient * gradient
    new_weight = weight - learn_rate * (new_one / (jnp.sqrt(new_two) + eps_adam) + weight_decay * weight)
    return (new_weight, new_one, new_two)

def product(left, right):
    return jnp.dot(left, right, preferred_element_type=jnp.float32, precision=lax.Precision.HIGHEST)

def attention(queries, key_rows, values, block_rows, scale_factor):
    seq_len = queries.shape[0]
    starts = (jnp.arange(seq_len // block_rows) * block_rows).astype(jnp.int32)

    def attend(row_start):
        query_block = lax.dynamic_slice_in_dim(queries, row_start, block_rows, 0)
        scores = low_back(jnp.einsum('qhd,khd->hqk', query_block, key_rows, precision=lax.Precision.HIGHEST) * scale_factor)
        allowed = (row_start + jnp.arange(block_rows))[:, None] >= jnp.arange(seq_len)[None, :]
        scores = jnp.where(allowed[None], scores, -1e+30)
        weights_low = low(jax.nn.softmax(scores, axis=-1))
        return jnp.einsum('hqk,khd->qhd', weights_low, values, precision=lax.Precision.HIGHEST)
    mixed_heads = lax.map(jax.checkpoint(attend), starts)
    return mixed_heads.reshape(seq_len, -1)

def block_layer(rows_in, flat_all):
    tensor_count = N_TENSOR
    heads_local = HEADS // tensor_count
    ff_local = FF // tensor_count
    width_local = D // tensor_count
    block_rows = min(512, SEQ_LEN)
    scale_factor = HD ** (-0.5)
    cosine, sine_table = rotary_tables(SEQ_LEN, ROT)
    pieces = [unpack(flat_all[tensor_rank], D, heads_local, ff_local, width_local) for tensor_rank in range(tensor_count)]
    norm_gains = jnp.concatenate([piece[4] for piece in pieces], axis=1)
    normed, inverse = layer_norm(rows_in)
    first_in = low(normed * norm_gains[0] + norm_gains[1])
    second_in = low(normed * norm_gains[2] + norm_gains[3])
    result = rows_in
    for tensor_rank in range(tensor_count):
        piece = pieces[tensor_rank]
        projected = low_back(product(low_back(first_in), piece[0])).reshape(SEQ_LEN, 3, heads_local, HD)
        queries = low(rotate(projected[:, 0], cosine, sine_table, ROT))
        key_rows = low(rotate(projected[:, 1], cosine, sine_table, ROT))
        values = low(projected[:, 2])
        attended = low(low_back(attention(queries, key_rows, values, block_rows, scale_factor)))
        hidden_pre = low_back(product(low_back(second_in), piece[2]))
        hidden_low = low(jax.nn.gelu(hidden_pre, approximate=False))
        result = result + low(product(attended, piece[1]) + product(hidden_low, piece[3]))
    return result

def reference(tokens, cotangent, seq_group, block_slot, master, first_moment, second_moment):
    heads_local = HEADS // N_TENSOR
    ff_local = FF // N_TENSOR
    block_count = block_slot.shape[0]
    params = low(master[:, block_slot, :]).reshape(N_TENSOR, -1)
    token_rows = tokens.astype(jnp.float32).reshape(N_DP, SEQ_DEV, SEQ_LEN, D)
    back_all = cotangent.astype(jnp.float32).reshape(N_DP, SEQ_DEV, SEQ_LEN, D)
    groups = seq_group.reshape(N_DP, SEQ_DEV)

    def one_sequence(pair):
        rows_in, back_rows = pair
        result, pullback = jax.vjp(block_layer, rows_in, params)
        grad_rows, grad_params = pullback(back_rows)
        return (result, grad_rows, grad_params)

    def one_device(accumulated, inputs):
        rows_in, back_rows, group_ids = inputs
        results, grad_rows, grad_params = lax.map(one_sequence, (rows_in, back_rows))
        member = (group_ids[None, :] == jnp.arange(SEQ_DEV, dtype=jnp.int32)[:, None]).astype(jnp.float32)
        group_grads = jnp.einsum('gs,stp->gtp', member, grad_params, precision=lax.Precision.HIGHEST)
        group_norms = jnp.sqrt(lax.optimization_barrier(jnp.sum(group_grads * group_grads, axis=(1, 2))))
        clip_scale = 1.0 / jnp.maximum(group_norms, 1.0)
        accumulated = accumulated + jnp.einsum('g,gtp->tp', clip_scale, group_grads, precision=lax.Precision.HIGHEST)
        return (accumulated, (results, grad_rows, group_norms))
    start_grad = jnp.zeros(params.shape, jnp.float32)
    total_grad, outs_all = lax.scan(one_device, start_grad, (token_rows, back_all, groups))
    results, grad_rows, group_norms = outs_all
    slot_total = N_DP * CAP
    slot_grad = jnp.zeros((N_TENSOR, slot_total, BLOCK_W), jnp.float32).at[:, block_slot, :].set(total_grad.reshape(N_TENSOR, block_count, BLOCK_W))
    slot_block = jnp.full((slot_total,), -1, jnp.int32).at[block_slot].set(jnp.arange(block_count, dtype=jnp.int32))
    position = jnp.maximum(slot_block, 0)[:, None] * BLOCK_W + jnp.arange(BLOCK_W, dtype=jnp.int32)[None, :]
    learn_rate, weight_decay = step_rates(position, D, heads_local, HD, ff_local, SEQ_LEN, FF)
    new_master, new_first, new_second = adam_update(master, first_moment, second_moment, slot_grad, learn_rate[None], weight_decay[None])
    return (results.reshape(TOKENS, D).astype(jnp.bfloat16), grad_rows.reshape(TOKENS, D), group_norms.reshape(-1), new_master, new_first, new_second)
```

```python
import functools
import jax
import jax.numpy as jnp
from jax import lax
from jax.experimental import pallas as pl
from jax.experimental.pallas import tpu as pltpu
from jax.sharding import PartitionSpec as P

HEADS = 12
HD = 64
ROT = 16
FF = 3072

eps_norm = 1e-05
eps_adam = 1e-08
beta_one = 0.5
beta_two = 0.6
root_half = 0.7071067811865476
inv_root_tau = 0.3989422804014327
PART = 256
VMEM_BYTES = 60 * 1024 * 1024


def dot_nn(left, right):
    return lax.dot_general(
        left, right, (((1,), (0,)), ((), ())), preferred_element_type=jnp.float32
    )


def dot_nt(left, right):
    return lax.dot_general(
        left, right, (((1,), (1,)), ((), ())), preferred_element_type=jnp.float32
    )


def dot_tn(left, right):
    return lax.dot_general(
        left, right, (((0,), (0,)), ((), ())), preferred_element_type=jnp.float32
    )


def turn_tables(seq_len):
    half = ROT // 2
    frequency = 10000.0 ** (-2.0 * jnp.arange(half, dtype=jnp.float32) / ROT)
    angles = jnp.arange(seq_len, dtype=jnp.float32)[:, None] * frequency[None, :]
    cosine, sine = jnp.cos(angles), jnp.sin(angles)
    rest = HD - ROT
    ones = jnp.ones((seq_len, rest), jnp.float32)
    zeros = jnp.zeros((seq_len, rest), jnp.float32)
    blank = jnp.zeros((seq_len, half), jnp.float32)
    keep = jnp.concatenate([cosine, cosine, ones], axis=1)
    low = jnp.concatenate([sine, blank, zeros], axis=1)
    high = jnp.concatenate([blank, sine, zeros], axis=1)
    return tuple(jnp.tile(t, (1, 128 // HD)) for t in (keep, low, high))


def turn(rows, keep, low, high, sign):
    half = ROT // 2
    pieces = []
    for start in range(0, rows.shape[1], 128):
        piece = rows[:, start : start + 128]
        ahead = pltpu.roll(piece, 128 - half, 1)
        behind = pltpu.roll(piece, half, 1)
        pieces.append(piece * keep + sign * (behind * high - ahead * low))
    return jnp.concatenate(pieces, axis=1)


def norm_rows(rows):
    mean = jnp.mean(rows, axis=-1, keepdims=True)
    centred = rows - mean
    inverse = lax.rsqrt(jnp.mean(centred * centred, axis=-1, keepdims=True) + eps_norm)
    return centred * inverse


def pair_squares(first, second):
    both = first + second
    parts = [both * both, first * first, second * second]
    return jnp.concatenate([jnp.sum(p, axis=0, keepdims=True) for p in parts], axis=0)


def dense_kernel(
    tiles_per_seq, x_ref, g_ref, wqkv_ref, wo_ref, wup_ref, wdn_ref, nrm_ref, keep_ref, low_ref, high_ref,
    q_ref, k_ref, v_ref, do_ref, hb_ref, e2_ref, gwd_ref, gwu_ref, gn_ref, sq_ref,
):
    step = pl.program_id(0)
    seq = step // tiles_per_seq

    @pl.when(step == 0)
    def _():
        gwd_ref[...] = jnp.zeros_like(gwd_ref)
        gwu_ref[...] = jnp.zeros_like(gwu_ref)
        gn_ref[...] = jnp.zeros_like(gn_ref)

    xhat = norm_rows(x_ref[...].astype(jnp.float32))
    first_in = (xhat * nrm_ref[0:1, :] + nrm_ref[1:2, :]).astype(jnp.bfloat16)
    second_in = (xhat * nrm_ref[2:3, :] + nrm_ref[3:4, :]).astype(jnp.bfloat16)
    back = g_ref[...]
    hidden_pre = dot_nn(second_in, wup_ref[...])
    grad_hidden = dot_nt(back, wdn_ref[...])
    cumulative = 0.5 * (1.0 + lax.erf(hidden_pre * root_half))
    density = jnp.exp(-0.5 * hidden_pre * hidden_pre) * inv_root_tau
    hidden = (hidden_pre * cumulative).astype(jnp.bfloat16)
    hb_ref[...] = hidden
    grad_pre = (grad_hidden * (cumulative + hidden_pre * density)).astype(jnp.bfloat16)
    projected = dot_nn(first_in, wqkv_ref[...])
    keep, low, high = keep_ref[...], low_ref[...], high_ref[...]
    q_ref[...] = (turn(projected[:, :PART], keep, low, high, 1.0) * HD ** (-0.5)).astype(jnp.bfloat16)
    k_ref[...] = turn(projected[:, PART : 2 * PART], keep, low, high, 1.0).astype(jnp.bfloat16)
    v_ref[...] = projected[:, 2 * PART :].astype(jnp.bfloat16)
    do_ref[...] = dot_nt(back, wo_ref[...]).astype(jnp.bfloat16)
    gwd_ref[seq] += dot_tn(hidden, back)
    gwu_ref[seq] += dot_tn(second_in, grad_pre)
    second_back = dot_nt(grad_pre, wup_ref[...]).astype(jnp.bfloat16)
    e2_ref[...] = second_back
    second_back = second_back.astype(jnp.float32)
    gn_ref[seq] += jnp.concatenate(
        [
            jnp.sum(second_back * xhat, axis=0, keepdims=True),
            jnp.sum(second_back, axis=0, keepdims=True),
        ],
        axis=0,
    )

    @pl.when(step == pl.num_programs(0) - 1)
    def _():
        sq_ref[...] = pair_squares(gwd_ref[0], gwd_ref[1]) + pair_squares(gwu_ref[0], gwu_ref[1])


def attend_kernel(
    block, heads, q_ref, k_ref, v_ref, do_ref, keep_ref, low_ref, high_ref,
    ao_ref, dq_ref, dk_ref, dv_ref, p_s, m_s, l_s, o_s, dq_s, dk_s, dv_s, qh_s, doh_s,
):
    i = pl.program_id(1)
    last = pl.num_programs(1) - 1

    @pl.when(i == 0)
    def _():
        dk_s[...] = jnp.zeros_like(dk_s)
        dv_s[...] = jnp.zeros_like(dv_s)

    dq_s[...] = jnp.zeros_like(dq_s)
    ao_ref[...] = jnp.zeros_like(ao_ref)
    lane_head = lax.broadcasted_iota(jnp.int32, (block, PART), 1) // HD

    def rows_of(j):
        return pl.ds(pl.multiple_of(j * block, block), block)

    def one_head(h, _):
        mine = lane_head == h
        zero = jnp.zeros((), jnp.bfloat16)
        q_head = jnp.where(mine, q_ref[...], zero)
        qh_s[...] = q_head
        do_head = jnp.where(mine, do_ref[...], zero)
        doh_s[...] = do_head
        scores = dot_nt(q_head, k_ref[rows_of(i), :])
        row = lax.broadcasted_iota(jnp.int32, (block, block), 0)
        col = lax.broadcasted_iota(jnp.int32, (block, block), 1)
        scores = jnp.where(row >= col, scores, -1e30)
        peak = jnp.max(scores, axis=1, keepdims=True)
        probs = jnp.exp(scores - peak)
        l_s[...] = jnp.broadcast_to(jnp.sum(probs, axis=1, keepdims=True), l_s.shape)
        probs = probs.astype(jnp.bfloat16)
        p_s[i] = probs
        m_s[i] = jnp.broadcast_to(peak, m_s.shape[1:])
        m_s[last + 1] = m_s[i]
        o_s[...] = dot_nn(probs, v_ref[rows_of(i), :])

        def ahead(j, _):
            scores = dot_nt(qh_s[...], k_ref[rows_of(j), :])
            before = m_s[last + 1][:, :1]
            peak = jnp.maximum(before, jnp.max(scores, axis=1, keepdims=True))
            fade = jnp.exp(before - peak)
            probs = jnp.exp(scores - peak)
            l_s[...] = l_s[...] * fade + jnp.sum(probs, axis=1, keepdims=True)
            probs = probs.astype(jnp.bfloat16)
            p_s[j] = probs
            wide = jnp.broadcast_to(peak, m_s.shape[1:])
            m_s[j] = wide
            m_s[last + 1] = wide
            o_s[...] = o_s[...] * fade + dot_nn(probs, v_ref[rows_of(j), :])
            return 0

        lax.fori_loop(0, i, ahead, 0)
        inverse = 1.0 / l_s[...]
        out = o_s[...] * inverse[:, :1]
        delta = jnp.sum(doh_s[...].astype(jnp.float32) * out, axis=1, keepdims=True)
        ao_ref[...] = jnp.where(mine, out.astype(jnp.bfloat16), ao_ref[...])
        l_s[...] = inverse
        o_s[:, :128] = jnp.broadcast_to(delta, (block, 128))

        def behind(j, _):
            scale = (jnp.exp(m_s[j] - m_s[last + 1]) * l_s[...])[:, :1]
            grad_out = (doh_s[...].astype(jnp.float32) * scale).astype(jnp.bfloat16)
            grad_probs = dot_nt(grad_out, v_ref[rows_of(j), :])
            probs = p_s[j]
            shift = o_s[:, :1] * scale
            grad_scores = (probs.astype(jnp.float32) * (grad_probs - shift)).astype(jnp.bfloat16)
            part = dot_nn(grad_scores, k_ref[rows_of(j), :])
            dq_s[...] += jnp.where(mine, part, 0.0)
            dk_s[rows_of(j), :] += dot_tn(grad_scores, qh_s[...])
            dv_s[rows_of(j), :] += dot_tn(probs, grad_out)
            return 0

        lax.fori_loop(0, i + 1, behind, 0)
        return 0

    lax.fori_loop(0, heads, one_head, 0)
    here = rows_of(i)
    dq_ref[...] = (
        turn(dq_s[...], keep_ref[here, :], low_ref[here, :], high_ref[here, :], -1.0) * HD ** (-0.5)
    ).astype(jnp.bfloat16)

    @pl.when(i == last)
    def _():
        dk_ref[...] = turn(dk_s[...], keep_ref[...], low_ref[...], high_ref[...], -1.0).astype(jnp.bfloat16)
        dv_ref[...] = dv_s[...].astype(jnp.bfloat16)


def grads_kernel(
    tiles_per_seq, x_ref, g_ref, ao_ref, dq_ref, dk_ref, dv_ref, wqkv_ref, nrm_ref,
    e1_ref, gwq_ref, gwo_ref, gn_ref, sq_ref,
):
    step = pl.program_id(0)
    seq = step // tiles_per_seq

    @pl.when(step == 0)
    def _():
        gwq_ref[...] = jnp.zeros_like(gwq_ref)
        gwo_ref[...] = jnp.zeros_like(gwo_ref)
        gn_ref[...] = jnp.zeros_like(gn_ref)

    xhat = norm_rows(x_ref[...].astype(jnp.float32))
    first_in = (xhat * nrm_ref[0:1, :] + nrm_ref[1:2, :]).astype(jnp.bfloat16)
    grad_qkv = jnp.concatenate([dq_ref[...], dk_ref[...], dv_ref[...]], axis=1)
    first_back = dot_nt(grad_qkv, wqkv_ref[...]).astype(jnp.bfloat16)
    e1_ref[...] = first_back
    gwq_ref[seq] += dot_tn(first_in, grad_qkv)
    gwo_ref[seq] += dot_tn(ao_ref[...], g_ref[...])
    first_back = first_back.astype(jnp.float32)
    gn_ref[seq] += jnp.concatenate(
        [
            jnp.sum(first_back * xhat, axis=0, keepdims=True),
            jnp.sum(first_back, axis=0, keepdims=True),
        ],
        axis=0,
    )

    @pl.when(step == pl.num_programs(0) - 1)
    def _():
        sq_ref[...] = pair_squares(gwq_ref[0], gwq_ref[1]) + pair_squares(gwo_ref[0], gwo_ref[1])


def branch_kernel(ao_ref, hb_ref, wo_ref, wdn_ref, br_ref):
    br_ref[...] = (dot_nn(ao_ref[...], wo_ref[...]) + dot_nn(hb_ref[...], wdn_ref[...])).astype(jnp.bfloat16)


def whole(shape):
    return pl.BlockSpec(shape, lambda *_: (0,) * len(shape))


def params(dims):
    return pltpu.CompilerParams(
        dimension_semantics=("arbitrary",) * dims, vmem_limit_bytes=VMEM_BYTES
    )


def dense(x_full, back_full, w_qkv, w_o, w_up, w_dn, norms, tables, seq_count, tile):
    rows, d = x_full.shape
    steps = rows // tile
    per_seq = steps // seq_count
    row = lambda width: pl.BlockSpec((tile, width), lambda s: (s, 0))
    table = pl.BlockSpec((tile, 128), lambda s: (lax.rem(s, per_seq), 0))
    act = lambda width: jax.ShapeDtypeStruct((rows, width), jnp.bfloat16)
    ff = w_up.shape[1]
    grad = jax.ShapeDtypeStruct((seq_count, ff, d), jnp.float32)
    grad_up = jax.ShapeDtypeStruct((seq_count, d, ff), jnp.float32)
    stat = jax.ShapeDtypeStruct((seq_count, 2, d), jnp.float32)
    squares = jax.ShapeDtypeStruct((3, d), jnp.float32)
    return pl.pallas_call(
        functools.partial(dense_kernel, per_seq),
        name="dense",
        grid=(steps,),
        in_specs=[row(d), row(d), whole(w_qkv.shape), whole(w_o.shape), whole(w_up.shape), whole(w_dn.shape),
                  whole(norms.shape), table, table, table],
        out_specs=[row(PART), row(PART), row(PART), row(PART), row(ff), row(d),
                   whole(grad.shape), whole(grad_up.shape), whole(stat.shape), whole(squares.shape)],
        out_shape=[act(PART), act(PART), act(PART), act(PART), act(ff), act(d), grad, grad_up, stat, squares],
        compiler_params=params(1),
    )(x_full, back_full, w_qkv, w_o, w_up, w_dn, norms, *tables)


def attend(q, k, v, d_out, tables, seq_count, block, heads):
    rows = q.shape[0]
    seq_len = rows // seq_count
    blocks = seq_len // block
    part = pl.BlockSpec((block, PART), lambda s, i: (s * blocks + i, 0))
    full = pl.BlockSpec((seq_len, PART), lambda s, i: (s, 0))
    act = jax.ShapeDtypeStruct((rows, PART), jnp.bfloat16)
    table = whole((seq_len, 128))
    return pl.pallas_call(
        functools.partial(attend_kernel, block, heads),
        name="attend",
        grid=(seq_count, blocks),
        in_specs=[part, full, full, part, table, table, table],
        out_specs=[part, part, full, full],
        out_shape=[act] * 4,
        scratch_shapes=[
            pltpu.VMEM((blocks, block, block), jnp.bfloat16),
            pltpu.VMEM((blocks + 1, block, 128), jnp.float32),
            pltpu.VMEM((block, 128), jnp.float32),
            pltpu.VMEM((block, PART), jnp.float32),
            pltpu.VMEM((block, PART), jnp.float32),
            pltpu.VMEM((seq_len, PART), jnp.float32),
            pltpu.VMEM((seq_len, PART), jnp.float32),
            pltpu.VMEM((block, PART), jnp.bfloat16),
            pltpu.VMEM((block, PART), jnp.bfloat16),
        ],
        compiler_params=params(2),
    )(q, k, v, d_out, *tables)


def grads(x_full, back_full, ao, dq, dk, dv, w_qkv, norms, seq_count, tile):
    rows, d = x_full.shape
    steps = rows // tile
    per_seq = steps // seq_count
    row = lambda width: pl.BlockSpec((tile, width), lambda s: (s, 0))
    grad_q = jax.ShapeDtypeStruct((seq_count, d, 3 * PART), jnp.float32)
    grad_o = jax.ShapeDtypeStruct((seq_count, PART, d), jnp.float32)
    stat = jax.ShapeDtypeStruct((seq_count, 2, d), jnp.float32)
    squares = jax.ShapeDtypeStruct((3, d), jnp.float32)
    return pl.pallas_call(
        functools.partial(grads_kernel, per_seq),
        name="grads",
        grid=(steps,),
        in_specs=[row(d), row(d), row(PART), row(PART), row(PART), row(PART), whole(w_qkv.shape), whole(norms.shape)],
        out_specs=[row(d), whole(grad_q.shape), whole(grad_o.shape), whole(stat.shape), whole(squares.shape)],
        out_shape=[jax.ShapeDtypeStruct((rows, d), jnp.bfloat16), grad_q, grad_o, stat, squares],
        compiler_params=params(1),
    )(x_full, back_full, ao, dq, dk, dv, w_qkv, norms)


def branch_of(ao, hb, w_o, w_dn, tile):
    rows = ao.shape[0]
    d = w_o.shape[1]
    row = lambda width: pl.BlockSpec((tile, width), lambda s: (s, 0))
    return pl.pallas_call(
        branch_kernel,
        name="branch",
        grid=(rows // tile,),
        in_specs=[row(ao.shape[1]), row(hb.shape[1]), whole(w_o.shape), whole(w_dn.shape)],
        out_specs=row(d),
        out_shape=jax.ShapeDtypeStruct((rows, d), jnp.bfloat16),
        compiler_params=params(1),
    )(ao, hb, w_o, w_dn)


def invert_kernel(slots_ref, out_ref):
    total = out_ref.shape[0]
    count = slots_ref.shape[0]
    wide = 16

    def clear(n, _):
        for u in range(wide):
            out_ref[n * wide + u] = -1
        return 0

    lax.fori_loop(0, total // wide, clear, 0)
    for n in range(total // wide * wide, total):
        out_ref[n] = -1

    def place(n, _):
        for u in range(wide):
            out_ref[slots_ref[n * wide + u]] = n * wide + u
        return 0

    lax.fori_loop(0, count // wide, place, 0)
    for n in range(count // wide * wide, count):
        out_ref[slots_ref[n]] = n


def invert(block_slot, total):
    return pl.pallas_call(
        invert_kernel,
        name="invert",
        in_specs=[pl.BlockSpec(memory_space=pltpu.SMEM)],
        out_specs=pl.BlockSpec(memory_space=pltpu.SMEM),
        out_shape=jax.ShapeDtypeStruct((total,), jnp.int32),
    )(block_slot)


def step_rates(position, d_model, inner_width, ff_local, seq_len):
    end_qkv = d_model * 3 * inner_width
    end_out = end_qkv + inner_width * d_model
    end_up = end_out + d_model * ff_local
    end_down = end_up + ff_local * d_model
    matrix_rate = d_model ** (-0.5)
    learn_rate = jnp.where(
        position < end_qkv,
        matrix_rate,
        jnp.where(
            position < end_out,
            (seq_len / (5.0 * d_model)) ** 0.5,
            jnp.where(position < end_up, matrix_rate, jnp.where(position < end_down, FF ** (-0.5), 0.1)),
        ),
    )
    weight_decay = jnp.where(position < end_down, 0.1, 0.0)
    return (learn_rate.astype(jnp.float32), weight_decay.astype(jnp.float32))


def on_device(tokens, cotangent, seq_group, block_slot, master, first_moment, second_moment):
    tensor_count = lax.axis_size("tensor")
    tensor_rank = lax.axis_index("tensor")
    owner_index = lax.axis_index("dp")
    owner_count = lax.axis_size("dp")
    local_rows, d = tokens.shape
    width_local = d // tensor_count
    heads_local = HEADS // tensor_count
    inner = heads_local * HD
    ff = FF // tensor_count
    seq_count = seq_group.shape[0]
    rows = local_rows * tensor_count
    seq_len = rows // seq_count
    capacity, block_width = master.shape[1:]
    block_count = block_slot.shape[0]
    slot_total = owner_count * capacity

    copies = lax.all_gather(master[0].astype(jnp.bfloat16), "dp", axis=0, tiled=True)
    slot_block = invert(block_slot, slot_total)
    x_full = lax.all_gather(tokens, "tensor", axis=0, tiled=True)
    back_full = lax.all_gather(cotangent, "tensor", axis=0, tiled=True)
    flat = copies[block_slot].reshape(-1)
    end_qkv = d * 3 * inner
    end_out = end_qkv + inner * d
    end_up = end_out + d * ff
    end_down = end_up + ff * d
    w_qkv = jnp.pad(flat[:end_qkv].reshape(d, 3, inner), ((0, 0), (0, 0), (0, PART - inner))).reshape(d, 3 * PART)
    w_o = jnp.pad(flat[end_qkv:end_out].reshape(inner, d), ((0, PART - inner), (0, 0)))
    w_up = flat[end_out:end_up].reshape(d, ff)
    w_dn = flat[end_up:end_down].reshape(ff, d)
    norm_rows_all = lax.all_gather(flat[end_down:].reshape(1, 4, width_local), "tensor", axis=0, tiled=True)
    norms = jnp.transpose(norm_rows_all, (1, 0, 2)).reshape(4, d).astype(jnp.float32)
    tables = turn_tables(seq_len)

    q, k, v, d_out, hidden, second_back, grad_down, grad_up, stat_two, squares_two = dense(
        x_full, back_full, w_qkv, w_o, w_up, w_dn, norms, tables, seq_count, 256
    )
    second_sum = lax.psum_scatter(second_back, "tensor", scatter_dimension=0, tiled=True)
    mixed, dq, dk, dv = attend(q, k, v, d_out, tables, seq_count, 512, heads_local)
    first_back, grad_qkv, grad_o, stat_one, squares_one = grads(
        x_full, back_full, mixed, dq, dk, dv, w_qkv, norms, seq_count, 256
    )
    branch = branch_of(mixed, hidden, w_o, w_dn, 512)

    local_squares = jnp.sum(squares_one + squares_two, axis=1)
    stats = jnp.concatenate([stat_one, stat_two], axis=1)
    packed = lax.psum(jnp.concatenate([stats.reshape(-1), local_squares]), "tensor")
    stats = packed[:-3].reshape(seq_count, 4, d)
    local_squares = packed[-3:]
    same = seq_group[0] == seq_group[1]
    stat_both = jnp.sum((stats[0] + stats[1]) ** 2)
    stat_each = jnp.sum(stats * stats, axis=(1, 2))
    each = local_squares[1:] + stat_each
    both = local_squares[0] + stat_both
    groups = jnp.arange(seq_count, dtype=jnp.int32)
    held = (seq_group[None, :] == groups[:, None]).astype(jnp.float32)
    sole = held[:, 0] * each[0] + held[:, 1] * each[1]
    norm_squares = jnp.where(held[:, 0] * held[:, 1] > 0, both, sole)
    group_norms = jnp.sqrt(norm_squares)
    clip = 1.0 / jnp.maximum(group_norms, 1.0)
    c = clip[seq_group]
    mix = lambda g: c[0] * g[0] + c[1] * g[1]
    own_stats = lax.dynamic_slice_in_dim(stats, tensor_rank * width_local, width_local, 2)
    clipped = jnp.concatenate(
        [
            mix(grad_qkv).reshape(d, 3, PART)[:, :, :inner].reshape(-1),
            mix(grad_o)[:inner].reshape(-1),
            mix(grad_up).reshape(-1),
            mix(grad_down).reshape(-1),
            mix(own_stats).reshape(-1),
        ]
    ).astype(jnp.bfloat16).reshape(block_count, block_width)
    padded = -(-capacity // 16) * 16
    wanted = jnp.pad(slot_block.reshape(owner_count, capacity), ((0, 0), (0, padded - capacity)), constant_values=-1)
    in_slots = clipped[jnp.maximum(wanted.reshape(-1), 0)]
    owned = lax.psum_scatter(in_slots, "dp", scatter_dimension=0, tiled=True)[:capacity].astype(jnp.float32)
    my_blocks = lax.dynamic_slice_in_dim(slot_block, owner_index * capacity, capacity)
    owned = jnp.where(my_blocks[:, None] >= 0, owned, 0.0)
    position = jnp.maximum(my_blocks, 0)[:, None] * block_width + jnp.arange(block_width, dtype=jnp.int32)[None, :]
    learn_rate, weight_decay = step_rates(position, d, inner, ff, seq_len)
    new_one = beta_one * first_moment[0] + (1.0 - beta_one) * owned
    new_two = beta_two * second_moment[0] + (1.0 - beta_two) * owned * owned
    new_weight = master[0] - learn_rate * (new_one / (jnp.sqrt(new_two) + eps_adam) + weight_decay * master[0])

    branch_sum = lax.psum_scatter(branch, "tensor", scatter_dimension=0, tiled=True).astype(jnp.float32)
    output = (tokens.astype(jnp.float32) + branch_sum).astype(jnp.bfloat16)
    first_sum = lax.psum_scatter(first_back, "tensor", scatter_dimension=0, tiled=True).astype(jnp.float32)
    second_sum = second_sum.astype(jnp.float32)
    own = tokens.astype(jnp.float32)
    centred = own - jnp.mean(own, axis=-1, keepdims=True)
    inverse = lax.rsqrt(jnp.mean(centred * centred, axis=-1, keepdims=True) + eps_norm)
    xhat = centred * inverse
    grad_input = cotangent.astype(jnp.float32)
    for total, gain in ((first_sum, norms[0]), (second_sum, norms[2])):
        scaled = total * gain
        mean = jnp.mean(scaled, axis=1, keepdims=True)
        cross = jnp.mean(scaled * xhat, axis=1, keepdims=True)
        grad_input = grad_input + inverse * (scaled - mean - xhat * cross)
    return (output, grad_input, group_norms, new_weight[None], new_one[None], new_two[None])


def solution(mesh):
    rows = P(("dp", "tensor"), None)
    slots = P("tensor", "dp", None)
    return jax.shard_map(
        on_device,
        mesh=mesh,
        in_specs=(rows, rows, P("dp"), P(), slots, slots, slots),
        out_specs=(rows, rows, P("dp"), slots, slots, slots),
        check_vma=False,
    )
```

```python
import functools
import jax
import jax.numpy as jnp
from jax import lax
from jax.experimental import pallas as pl
from jax.experimental.pallas import tpu as pltpu
from jax.sharding import PartitionSpec as P

HEADS = 12
HD = 64
ROT = 16
FF = 3072

eps_norm = 1e-05
eps_adam = 1e-08
beta_one = 0.5
beta_two = 0.6
root_half = 0.7071067811865476
inv_root_tau = 0.3989422804014327
PART = 256
VMEM_BYTES = 60 * 1024 * 1024


def dot_nn(left, right):
    return lax.dot_general(
        left, right, (((1,), (0,)), ((), ())), preferred_element_type=jnp.float32
    )


def dot_nt(left, right):
    return lax.dot_general(
        left, right, (((1,), (1,)), ((), ())), preferred_element_type=jnp.float32
    )


def dot_tn(left, right):
    return lax.dot_general(
        left, right, (((0,), (0,)), ((), ())), preferred_element_type=jnp.float32
    )


def turn_tables(seq_len):
    half = ROT // 2
    frequency = 10000.0 ** (-2.0 * jnp.arange(half, dtype=jnp.float32) / ROT)
    angles = jnp.arange(seq_len, dtype=jnp.float32)[:, None] * frequency[None, :]
    cosine, sine = jnp.cos(angles), jnp.sin(angles)
    rest = HD - ROT
    ones = jnp.ones((seq_len, rest), jnp.float32)
    zeros = jnp.zeros((seq_len, rest), jnp.float32)
    blank = jnp.zeros((seq_len, half), jnp.float32)
    keep = jnp.concatenate([cosine, cosine, ones], axis=1)
    low = jnp.concatenate([sine, blank, zeros], axis=1)
    high = jnp.concatenate([blank, sine, zeros], axis=1)
    return tuple(jnp.tile(t, (1, 128 // HD)) for t in (keep, low, high))


def turn(rows, keep, low, high, sign):
    half = ROT // 2
    pieces = []
    for start in range(0, rows.shape[1], 128):
        piece = rows[:, start : start + 128]
        ahead = pltpu.roll(piece, 128 - half, 1)
        behind = pltpu.roll(piece, half, 1)
        pieces.append(piece * keep + sign * (behind * high - ahead * low))
    return jnp.concatenate(pieces, axis=1)


def norm_rows(rows):
    mean = jnp.mean(rows, axis=-1, keepdims=True)
    centred = rows - mean
    inverse = lax.rsqrt(jnp.mean(centred * centred, axis=-1, keepdims=True) + eps_norm)
    return centred * inverse


def pair_squares(first, second):
    both = first + second
    parts = [both * both, first * first, second * second]
    return jnp.concatenate([jnp.sum(p, axis=0, keepdims=True) for p in parts], axis=0)


def pick(place, own, near, far, both):
    low = jnp.where(place == 0, own[...], near[...])
    high = jnp.where(place == 2, far[...], both[...])
    return jnp.where(place < 2, low, high)


def put_pair(place, rows, stay_ref, give_ref):
    @pl.when(place % 2 == 0)
    def _():
        stay_ref[...] = rows

    @pl.when(place % 2 == 1)
    def _():
        give_ref[...] = rows


def piece_specs(tile, width, per_piece):
    def at(n):
        def index(step, core_ref):
            return (jnp.where(((step // per_piece) ^ core_ref[0]) == n, step % per_piece, 0), 0)

        return pl.BlockSpec((tile, width), index)

    return [at(n) for n in range(4)]


def pair_specs(tile, width, per_piece):
    def at(parity):
        def index(step, core_ref):
            piece = step // per_piece
            first = piece // 2 * per_piece
            idle = jnp.where(piece % 2 == 1, first + per_piece - 1, jnp.maximum(first - 1, 0))
            return (jnp.where((piece ^ core_ref[0]) % 2 == parity, first + step % per_piece, idle), 0)

        return pl.BlockSpec((tile, width), index)

    return [at(0), at(1)]


def dense_kernel(
    tiles_per_seq, core_ref, x0_ref, x1_ref, x2_ref, x3_ref, g0_ref, g1_ref, g2_ref, g3_ref,
    wqkv_ref, wo_ref, wup_ref, wdn_ref, nrm_ref, keep_ref, low_ref, high_ref,
    q_ref, k_ref, v_ref, do_ref, hb_ref, stay_ref, give_ref, gwd_ref, gwu_ref, gn_ref, sq_ref,
):
    step = pl.program_id(0)
    seq = step // tiles_per_seq
    place = (2 * step // tiles_per_seq) ^ core_ref[0]

    @pl.when(step == 0)
    def _():
        gwd_ref[...] = jnp.zeros_like(gwd_ref)
        gwu_ref[...] = jnp.zeros_like(gwu_ref)
        gn_ref[...] = jnp.zeros_like(gn_ref)

    xhat = norm_rows(pick(place, x0_ref, x1_ref, x2_ref, x3_ref).astype(jnp.float32))
    first_in = (xhat * nrm_ref[0:1, :] + nrm_ref[1:2, :]).astype(jnp.bfloat16)
    second_in = (xhat * nrm_ref[2:3, :] + nrm_ref[3:4, :]).astype(jnp.bfloat16)
    back = pick(place, g0_ref, g1_ref, g2_ref, g3_ref)
    hidden_pre = dot_nn(second_in, wup_ref[...])
    grad_hidden = dot_nt(back, wdn_ref[...])
    cumulative = 0.5 * (1.0 + lax.erf(hidden_pre * root_half))
    density = jnp.exp(-0.5 * hidden_pre * hidden_pre) * inv_root_tau
    hidden = (hidden_pre * cumulative).astype(jnp.bfloat16)
    hb_ref[...] = hidden
    grad_pre = (grad_hidden * (cumulative + hidden_pre * density)).astype(jnp.bfloat16)
    projected = dot_nn(first_in, wqkv_ref[...])
    keep, low, high = keep_ref[...], low_ref[...], high_ref[...]
    q_ref[...] = (turn(projected[:, :PART], keep, low, high, 1.0) * HD ** (-0.5)).astype(jnp.bfloat16)
    k_ref[...] = turn(projected[:, PART : 2 * PART], keep, low, high, 1.0).astype(jnp.bfloat16)
    v_ref[...] = projected[:, 2 * PART :].astype(jnp.bfloat16)
    do_ref[...] = dot_nt(back, wo_ref[...]).astype(jnp.bfloat16)
    gwd_ref[seq] += dot_tn(hidden, back)
    gwu_ref[seq] += dot_tn(second_in, grad_pre)
    second_back = dot_nt(grad_pre, wup_ref[...]).astype(jnp.bfloat16)
    put_pair(place, second_back, stay_ref, give_ref)
    second_back = second_back.astype(jnp.float32)
    gn_ref[seq] += jnp.concatenate(
        [
            jnp.sum(second_back * xhat, axis=0, keepdims=True),
            jnp.sum(second_back, axis=0, keepdims=True),
        ],
        axis=0,
    )

    @pl.when(step == pl.num_programs(0) - 1)
    def _():
        sq_ref[...] = pair_squares(gwd_ref[0], gwd_ref[1]) + pair_squares(gwu_ref[0], gwu_ref[1])


def attend_kernel(
    block, heads, q_ref, k_ref, v_ref, do_ref, keep_ref, low_ref, high_ref,
    ao_ref, dq_ref, dk_ref, dv_ref, p_s, m_s, l_s, o_s, dq_s, dk_s, dv_s, qh_s, doh_s,
):
    i = pl.program_id(1)
    last = pl.num_programs(1) - 1

    @pl.when(i == 0)
    def _():
        dk_s[...] = jnp.zeros_like(dk_s)
        dv_s[...] = jnp.zeros_like(dv_s)

    dq_s[...] = jnp.zeros_like(dq_s)
    ao_ref[...] = jnp.zeros_like(ao_ref)
    lane_head = lax.broadcasted_iota(jnp.int32, (block, PART), 1) // HD

    def rows_of(j):
        return pl.ds(pl.multiple_of(j * block, block), block)

    def one_head(h, _):
        mine = lane_head == h
        zero = jnp.zeros((), jnp.bfloat16)
        q_head = jnp.where(mine, q_ref[...], zero)
        qh_s[...] = q_head
        do_head = jnp.where(mine, do_ref[...], zero)
        doh_s[...] = do_head
        scores = dot_nt(q_head, k_ref[rows_of(i), :])
        row = lax.broadcasted_iota(jnp.int32, (block, block), 0)
        col = lax.broadcasted_iota(jnp.int32, (block, block), 1)
        scores = jnp.where(row >= col, scores, -1e30)
        peak = jnp.max(scores, axis=1, keepdims=True)
        probs = jnp.exp(scores - peak)
        l_s[...] = jnp.broadcast_to(jnp.sum(probs, axis=1, keepdims=True), l_s.shape)
        probs = probs.astype(jnp.bfloat16)
        p_s[i] = probs
        m_s[i] = jnp.broadcast_to(peak, m_s.shape[1:])
        m_s[last + 1] = m_s[i]
        o_s[...] = dot_nn(probs, v_ref[rows_of(i), :])

        def ahead(j, _):
            scores = dot_nt(qh_s[...], k_ref[rows_of(j), :])
            before = m_s[last + 1][:, :1]
            peak = jnp.maximum(before, jnp.max(scores, axis=1, keepdims=True))
            fade = jnp.exp(before - peak)
            probs = jnp.exp(scores - peak)
            l_s[...] = l_s[...] * fade + jnp.sum(probs, axis=1, keepdims=True)
            probs = probs.astype(jnp.bfloat16)
            p_s[j] = probs
            wide = jnp.broadcast_to(peak, m_s.shape[1:])
            m_s[j] = wide
            m_s[last + 1] = wide
            o_s[...] = o_s[...] * fade + dot_nn(probs, v_ref[rows_of(j), :])
            return 0

        lax.fori_loop(0, i, ahead, 0)
        inverse = 1.0 / l_s[...]
        out = o_s[...] * inverse[:, :1]
        delta = jnp.sum(doh_s[...].astype(jnp.float32) * out, axis=1, keepdims=True)
        ao_ref[...] = jnp.where(mine, out.astype(jnp.bfloat16), ao_ref[...])
        l_s[...] = inverse
        o_s[:, :128] = jnp.broadcast_to(delta, (block, 128))

        def behind(j, _):
            scale = (jnp.exp(m_s[j] - m_s[last + 1]) * l_s[...])[:, :1]
            grad_out = (doh_s[...].astype(jnp.float32) * scale).astype(jnp.bfloat16)
            grad_probs = dot_nt(grad_out, v_ref[rows_of(j), :])
            probs = p_s[j]
            shift = o_s[:, :1] * scale
            grad_scores = (probs.astype(jnp.float32) * (grad_probs - shift)).astype(jnp.bfloat16)
            part = dot_nn(grad_scores, k_ref[rows_of(j), :])
            dq_s[...] += jnp.where(mine, part, 0.0)
            dk_s[rows_of(j), :] += dot_tn(grad_scores, qh_s[...])
            dv_s[rows_of(j), :] += dot_tn(probs, grad_out)
            return 0

        lax.fori_loop(0, i + 1, behind, 0)
        return 0

    lax.fori_loop(0, heads, one_head, 0)
    here = rows_of(i)
    dq_ref[...] = (
        turn(dq_s[...], keep_ref[here, :], low_ref[here, :], high_ref[here, :], -1.0) * HD ** (-0.5)
    ).astype(jnp.bfloat16)

    @pl.when(i == last)
    def _():
        dk_ref[...] = turn(dk_s[...], keep_ref[...], low_ref[...], high_ref[...], -1.0).astype(jnp.bfloat16)
        dv_ref[...] = dv_s[...].astype(jnp.bfloat16)


def grads_kernel(
    tiles_per_seq, core_ref, x0_ref, x1_ref, x2_ref, x3_ref, g0_ref, g1_ref, g2_ref, g3_ref,
    ao_ref, dq_ref, dk_ref, dv_ref, wqkv_ref, nrm_ref,
    stay_ref, give_ref, gwq_ref, gwo_ref, gn_ref, sq_ref,
):
    step = pl.program_id(0)
    seq = step // tiles_per_seq
    place = (2 * step // tiles_per_seq) ^ core_ref[0]

    @pl.when(step == 0)
    def _():
        gwq_ref[...] = jnp.zeros_like(gwq_ref)
        gwo_ref[...] = jnp.zeros_like(gwo_ref)
        gn_ref[...] = jnp.zeros_like(gn_ref)

    xhat = norm_rows(pick(place, x0_ref, x1_ref, x2_ref, x3_ref).astype(jnp.float32))
    first_in = (xhat * nrm_ref[0:1, :] + nrm_ref[1:2, :]).astype(jnp.bfloat16)
    grad_qkv = jnp.concatenate([dq_ref[...], dk_ref[...], dv_ref[...]], axis=1)
    first_back = dot_nt(grad_qkv, wqkv_ref[...]).astype(jnp.bfloat16)
    put_pair(place, first_back, stay_ref, give_ref)
    gwq_ref[seq] += dot_tn(first_in, grad_qkv)
    gwo_ref[seq] += dot_tn(ao_ref[...], pick(place, g0_ref, g1_ref, g2_ref, g3_ref))
    first_back = first_back.astype(jnp.float32)
    gn_ref[seq] += jnp.concatenate(
        [
            jnp.sum(first_back * xhat, axis=0, keepdims=True),
            jnp.sum(first_back, axis=0, keepdims=True),
        ],
        axis=0,
    )

    @pl.when(step == pl.num_programs(0) - 1)
    def _():
        sq_ref[...] = pair_squares(gwq_ref[0], gwq_ref[1]) + pair_squares(gwo_ref[0], gwo_ref[1])


def branch_kernel(per_piece, core_ref, ao_ref, hb_ref, wo_ref, wdn_ref, stay_ref, give_ref):
    place = (pl.program_id(0) // per_piece) ^ core_ref[0]
    rows = (dot_nn(ao_ref[...], wo_ref[...]) + dot_nn(hb_ref[...], wdn_ref[...])).astype(jnp.bfloat16)
    put_pair(place, rows, stay_ref, give_ref)


def whole(shape):
    return pl.BlockSpec(shape, lambda *_: (0,) * len(shape))


def params(dims):
    return pltpu.CompilerParams(
        dimension_semantics=("arbitrary",) * dims, vmem_limit_bytes=VMEM_BYTES
    )


def dense(core, x_parts, back_parts, w_qkv, w_o, w_up, w_dn, norms, tables, seq_count, tile):
    rows, d = 4 * x_parts[0].shape[0], x_parts[0].shape[1]
    steps = rows // tile
    per_seq = steps // seq_count
    row = lambda width: pl.BlockSpec((tile, width), lambda s, _: (s, 0))
    table = pl.BlockSpec((tile, 128), lambda s, _: (lax.rem(s, per_seq), 0))
    act = lambda width: jax.ShapeDtypeStruct((rows, width), jnp.bfloat16)
    pair = jax.ShapeDtypeStruct((rows // 2, d), jnp.bfloat16)
    ff = w_up.shape[1]
    grad = jax.ShapeDtypeStruct((seq_count, ff, d), jnp.float32)
    grad_up = jax.ShapeDtypeStruct((seq_count, d, ff), jnp.float32)
    stat = jax.ShapeDtypeStruct((seq_count, 2, d), jnp.float32)
    squares = jax.ShapeDtypeStruct((3, d), jnp.float32)
    pieces = piece_specs(tile, d, steps // 4)
    return pl.pallas_call(
        functools.partial(dense_kernel, per_seq),
        name="dense",
        grid_spec=pltpu.PrefetchScalarGridSpec(
            num_scalar_prefetch=1,
            grid=(steps,),
            in_specs=pieces + pieces + [whole(w_qkv.shape), whole(w_o.shape), whole(w_up.shape), whole(w_dn.shape),
                                        whole(norms.shape), table, table, table],
            out_specs=[row(PART), row(PART), row(PART), row(PART), row(ff)] + pair_specs(tile, d, steps // 4)
            + [whole(grad.shape), whole(grad_up.shape), whole(stat.shape), whole(squares.shape)],
        ),
        out_shape=[act(PART), act(PART), act(PART), act(PART), act(ff), pair, pair, grad, grad_up, stat, squares],
        compiler_params=params(1),
    )(core, *x_parts, *back_parts, w_qkv, w_o, w_up, w_dn, norms, *tables)


def attend(q, k, v, d_out, tables, seq_count, block, heads):
    rows = q.shape[0]
    seq_len = rows // seq_count
    blocks = seq_len // block
    part = pl.BlockSpec((block, PART), lambda s, i: (s * blocks + i, 0))
    full = pl.BlockSpec((seq_len, PART), lambda s, i: (s, 0))
    act = jax.ShapeDtypeStruct((rows, PART), jnp.bfloat16)
    table = whole((seq_len, 128))
    return pl.pallas_call(
        functools.partial(attend_kernel, block, heads),
        name="attend",
        grid=(seq_count, blocks),
        in_specs=[part, full, full, part, table, table, table],
        out_specs=[part, part, full, full],
        out_shape=[act] * 4,
        scratch_shapes=[
            pltpu.VMEM((blocks, block, block), jnp.bfloat16),
            pltpu.VMEM((blocks + 1, block, 128), jnp.float32),
            pltpu.VMEM((block, 128), jnp.float32),
            pltpu.VMEM((block, PART), jnp.float32),
            pltpu.VMEM((block, PART), jnp.float32),
            pltpu.VMEM((seq_len, PART), jnp.float32),
            pltpu.VMEM((seq_len, PART), jnp.float32),
            pltpu.VMEM((block, PART), jnp.bfloat16),
            pltpu.VMEM((block, PART), jnp.bfloat16),
        ],
        compiler_params=params(2),
    )(q, k, v, d_out, *tables)


def grads(core, x_parts, back_parts, ao, dq, dk, dv, w_qkv, norms, seq_count, tile):
    rows, d = 4 * x_parts[0].shape[0], x_parts[0].shape[1]
    steps = rows // tile
    per_seq = steps // seq_count
    row = lambda width: pl.BlockSpec((tile, width), lambda s, _: (s, 0))
    pair = jax.ShapeDtypeStruct((rows // 2, d), jnp.bfloat16)
    grad_q = jax.ShapeDtypeStruct((seq_count, d, 3 * PART), jnp.float32)
    grad_o = jax.ShapeDtypeStruct((seq_count, PART, d), jnp.float32)
    stat = jax.ShapeDtypeStruct((seq_count, 2, d), jnp.float32)
    squares = jax.ShapeDtypeStruct((3, d), jnp.float32)
    pieces = piece_specs(tile, d, steps // 4)
    return pl.pallas_call(
        functools.partial(grads_kernel, per_seq),
        name="grads",
        grid_spec=pltpu.PrefetchScalarGridSpec(
            num_scalar_prefetch=1,
            grid=(steps,),
            in_specs=pieces + pieces + [row(PART)] * 4 + [whole(w_qkv.shape), whole(norms.shape)],
            out_specs=pair_specs(tile, d, steps // 4)
            + [whole(grad_q.shape), whole(grad_o.shape), whole(stat.shape), whole(squares.shape)],
        ),
        out_shape=[pair, pair, grad_q, grad_o, stat, squares],
        compiler_params=params(1),
    )(core, *x_parts, *back_parts, ao, dq, dk, dv, w_qkv, norms)


def branch_of(core, ao, hb, w_o, w_dn, tile):
    rows = ao.shape[0]
    d = w_o.shape[1]
    row = lambda width: pl.BlockSpec((tile, width), lambda s, _: (s, 0))
    pair = jax.ShapeDtypeStruct((rows // 2, d), jnp.bfloat16)
    return pl.pallas_call(
        functools.partial(branch_kernel, rows // tile // 4),
        name="branch",
        grid_spec=pltpu.PrefetchScalarGridSpec(
            num_scalar_prefetch=1,
            grid=(rows // tile,),
            in_specs=[row(ao.shape[1]), row(hb.shape[1]), whole(w_o.shape), whole(w_dn.shape)],
            out_specs=pair_specs(tile, d, rows // tile // 4),
        ),
        out_shape=[pair, pair],
        compiler_params=params(1),
    )(core, ao, hb, w_o, w_dn)


def swap_halves(piece):
    return pltpu.roll(piece, 64, 1)


def unpack_kernel(spans, counts, starts_ref, slots_ref, *refs):
    arrays = refs[: len(spans)]
    wqkv_ref, wo_ref, wup_ref, wdn_ref, nrm_ref, table_s, flat_s, wide_s = refs[len(spans) :]
    d, inner, ff = counts
    for n, (array, span) in enumerate(zip(arrays, spans)):
        start = starts_ref[n]

        @pl.when(start >= 0)
        def _():
            table_s[pl.ds(pl.multiple_of(start, 16), span), :] = array[...].astype(jnp.float32)

    blocks = slots_ref.shape[0]
    wide = 16

    def fetch(n, _):
        for u in range(wide):
            b = n * wide + u
            flat_s[pl.ds(b, 1), :] = table_s[pl.ds(slots_ref[b], 1), :]
        return 0

    lax.fori_loop(0, blocks // wide, fetch, 0)
    for b in range(blocks // wide * wide, blocks):
        flat_s[pl.ds(b, 1), :] = table_s[pl.ds(slots_ref[b], 1), :]

    half = lax.broadcasted_iota(jnp.int32, (d // 2, 128), 1) < 64
    e = [flat_s[pl.ds(c, d // 2, stride=9), :] for c in range(9)]
    even = [
        e[0], jnp.where(half, e[1], 0.0),
        jnp.where(half, swap_halves(e[1]), swap_halves(e[2])), jnp.where(half, swap_halves(e[2]), 0.0),
        e[3], jnp.where(half, e[4], 0.0),
    ]
    odd = [
        jnp.where(half, swap_halves(e[4]), swap_halves(e[5])), jnp.where(half, swap_halves(e[5]), 0.0),
        e[6], jnp.where(half, e[7], 0.0),
        jnp.where(half, swap_halves(e[7]), swap_halves(e[8])), jnp.where(half, swap_halves(e[8]), 0.0),
    ]
    for c in range(6):
        wide_s[pl.ds(0, d // 2, stride=2), :] = even[c]
        wide_s[pl.ds(1, d // 2, stride=2), :] = odd[c]
        wqkv_ref[:, c * 128 : (c + 1) * 128] = wide_s[...].astype(jnp.bfloat16)
    base = d * 3 * inner // 128
    step = d // 128
    for ref, height in ((wo_ref, inner), (wup_ref, d), (wdn_ref, ff)):
        for c in range(step):
            ref[:height, c * 128 : (c + 1) * 128] = flat_s[pl.ds(base + c, height, stride=step), :].astype(jnp.bfloat16)
        base += height * step
    wo_ref[inner:, :] = jnp.zeros_like(wo_ref[inner:, :])
    nrm_ref[...] = flat_s[pl.ds(base, blocks - base), :].astype(jnp.bfloat16)


def unpack(arrays, starts, slots, table_rows, d, inner, ff):
    spans = tuple(a.shape[0] for a in arrays)
    blocks = slots.shape[0]
    smem = pl.BlockSpec(memory_space=pltpu.SMEM)
    vmem = pl.BlockSpec(memory_space=pltpu.VMEM)
    end = (d * 3 * inner + inner * d + 2 * d * ff) // 128
    weight = lambda h, w: jax.ShapeDtypeStruct((h, w), jnp.bfloat16)
    return pl.pallas_call(
        functools.partial(unpack_kernel, spans, (d, inner, ff)),
        name="unpack",
        in_specs=[smem, smem] + [vmem] * len(arrays),
        out_specs=[vmem] * 5,
        out_shape=[weight(d, 3 * PART), weight(PART, d), weight(d, ff), weight(ff, d), weight(blocks - end, 128)],
        scratch_shapes=[
            pltpu.VMEM((table_rows, 128), jnp.float32),
            pltpu.VMEM((-(-blocks // 16) * 16, 128), jnp.float32),
            pltpu.VMEM((d, 128), jnp.float32),
        ],
        compiler_params=pltpu.CompilerParams(vmem_limit_bytes=VMEM_BYTES),
    )(starts, slots, *arrays)


def pack_kernel(spans, counts, starts_ref, slots_ref, clip_ref, gwq_ref, gwo_ref, gwu_ref, gwd_ref, stat_ref, *refs):
    outs = refs[: len(spans)]
    flat_s, slot_s, wide_s = refs[len(spans) :]
    d, inner, ff = counts
    one, two = clip_ref[0], clip_ref[1]
    half = lax.broadcasted_iota(jnp.int32, (d // 2, 128), 1) < 64
    even, odd = [], []
    for c in range(6):
        cols = slice(c * 128, (c + 1) * 128)
        wide_s[c] = gwq_ref[0, :, cols] * one + gwq_ref[1, :, cols] * two
        even.append(wide_s[c, pl.ds(0, d // 2, stride=2), :])
        odd.append(wide_s[c, pl.ds(1, d // 2, stride=2), :])
    q0, q1, k0, k1, v0, v1 = even
    r0, r1, s0, s1, u0, u1 = odd
    pieces = [
        q0, jnp.where(half, q1, swap_halves(k0)), jnp.where(half, swap_halves(k0), swap_halves(k1)),
        v0, jnp.where(half, v1, swap_halves(r0)), jnp.where(half, swap_halves(r0), swap_halves(r1)),
        s0, jnp.where(half, s1, swap_halves(u0)), jnp.where(half, swap_halves(u0), swap_halves(u1)),
    ]
    for c in range(9):
        flat_s[pl.ds(c, d // 2, stride=9), :] = pieces[c]
    base = d * 3 * inner // 128
    step = d // 128
    for ref, height in ((gwo_ref, inner), (gwu_ref, d), (gwd_ref, ff)):
        for c in range(step):
            cols = slice(c * 128, (c + 1) * 128)
            flat_s[pl.ds(base + c, height, stride=step), :] = ref[0, :height, cols] * one + ref[1, :height, cols] * two
        base += height * step
    blocks = slots_ref.shape[0]
    flat_s[pl.ds(base, blocks - base), :] = stat_ref[...]
    wide = 16

    def place(n, _):
        for u in range(wide):
            b = n * wide + u
            slot_s[pl.ds(slots_ref[b], 1), :] = flat_s[pl.ds(b, 1), :]
        return 0

    lax.fori_loop(0, blocks // wide, place, 0)
    for b in range(blocks // wide * wide, blocks):
        slot_s[pl.ds(slots_ref[b], 1), :] = flat_s[pl.ds(b, 1), :]
    for n, (out, span) in enumerate(zip(outs, spans)):
        out[...] = slot_s[pl.ds(pl.multiple_of(starts_ref[n], 16), span), :].astype(jnp.bfloat16)


def pack(grad_qkv, grad_o, grad_up, grad_down, stat, clip, slots, starts, spans, table_rows, d, inner, ff):
    blocks = slots.shape[0]
    smem = pl.BlockSpec(memory_space=pltpu.SMEM)
    vmem = pl.BlockSpec(memory_space=pltpu.VMEM)
    return pl.pallas_call(
        functools.partial(pack_kernel, spans, (d, inner, ff)),
        name="pack",
        in_specs=[smem] * 3 + [vmem] * 5,
        out_specs=[vmem] * len(spans),
        out_shape=[jax.ShapeDtypeStruct((s, 128), jnp.bfloat16) for s in spans],
        scratch_shapes=[
            pltpu.VMEM((-(-blocks // 16) * 16, 128), jnp.float32),
            pltpu.VMEM((table_rows, 128), jnp.float32),
            pltpu.VMEM((6, d, 128), jnp.float32),
        ],
        compiler_params=pltpu.CompilerParams(vmem_limit_bytes=VMEM_BYTES),
    )(starts, slots, clip, grad_qkv, grad_o, grad_up, grad_down, stat)


def ladder(step, test, outer):
    return [
        (2 * z + x, 2 * (z + step) + x) for z in range(outer) for x in range(2) if test(z) and 0 <= z + step < outer
    ]


def cross(test, outer):
    return [(2 * z + x, 2 * z + 1 - x) for z in range(outer) for x in range(2) if test(z)]


def collect_slots(own, owner_index, owner_count, span):
    if owner_count != 8:
        return [lax.all_gather(own, "dp", axis=0, tiled=True)], jnp.zeros((1,), jnp.int32)
    z, x = owner_index // 2, owner_index % 2
    arrays = [own, lax.ppermute(own, "dp", cross(lambda q: True, 4))]
    owners = [2 * z + x, 2 * z + 1 - x]
    up = down = own
    for hop in range(3):
        up = lax.ppermute(up, "dp", ladder(1, lambda q: q >= hop, 4))
        down = lax.ppermute(down, "dp", ladder(-1, lambda q: q <= 3 - hop, 4))
        up_x = lax.ppermute(up, "dp", cross(lambda q: q > hop, 4))
        down_x = lax.ppermute(down, "dp", cross(lambda q: q < 3 - hop, 4))
        arrays += [up, down, up_x, down_x]
        low, high = z - 1 - hop, z + 1 + hop
        for there, has in ((low, low >= 0), (high, high < 4)):
            owners.append(jnp.where(has, 2 * there + x, -1))
        for there, has in ((low, low >= 0), (high, high < 4)):
            owners.append(jnp.where(has, 2 * there + 1 - x, -1))
    owners = jnp.stack(owners)
    return arrays, jnp.where(owners >= 0, owners * span, -1).astype(jnp.int32)


def pack_starts(owner_index, owner_count, span):
    if owner_count != 8:
        return (owner_count * span,), jnp.zeros((1,), jnp.int32)
    z, x = owner_index // 2, owner_index % 2
    order = jnp.array([[3, 2, 1, 0], [3, 0, 2, 1], [0, 3, 1, 2], [0, 1, 2, 3]], jnp.int32)[z]
    return (span,) * 8, jnp.concatenate([2 * order + 1 - x, 2 * order + x]).astype(jnp.int32) * span


def sum_to_owners(packed, owner_index, owner_count):
    if owner_count != 8:
        return lax.psum_scatter(packed[0], "dp", scatter_dimension=0, tiled=True)
    z = owner_index // 2
    part = [mine + lax.ppermute(give, "dp", cross(lambda q: True, 4)) for give, mine in zip(packed[:4], packed[4:])]
    up = lax.ppermute(part[0], "dp", ladder(1, lambda q: q == 0, 4))
    down = lax.ppermute(part[0], "dp", ladder(-1, lambda q: q == 3, 4))
    middle = jnp.where((z == 0) | (z == 3), part[1], part[0])
    up = lax.ppermute(middle + up, "dp", ladder(1, lambda q: q <= 1, 4))
    down = lax.ppermute(middle + down, "dp", ladder(-1, lambda q: q >= 2, 4))
    up = lax.ppermute(jnp.where(z == 2, part[1], part[2]) + up, "dp", ladder(1, lambda q: q <= 2, 4))
    down = lax.ppermute(jnp.where(z == 1, part[1], part[2]) + down, "dp", ladder(-1, lambda q: q >= 1, 4))
    return part[3] + up + down


NEAR = [(i, i ^ 1) for i in range(4)]
FAR = [(i, i ^ 2) for i in range(4)]


def meet(stay, give):
    got = lax.ppermute(give, "tensor", NEAR)
    both = stay.astype(jnp.float32) + got.astype(jnp.float32)
    rows = stay.shape[0] // 2
    return both[:rows], both[rows:].astype(jnp.bfloat16)


def close(kept, sent):
    return kept + lax.ppermute(sent, "tensor", FAR).astype(jnp.float32)


def slot_classes(slots, first, capacity, ends):
    block = jnp.arange(slots.shape[0], dtype=jnp.int32)
    code = jnp.where(block < ends[0], 1, jnp.where(block < ends[1], 2, jnp.where(block < ends[2], 1, jnp.where(block < ends[3], 3, 4))))
    at = slots - first
    high = jnp.arange(-(-capacity // 128), dtype=jnp.int32)
    inside = (at >= 0) & (at < capacity)
    tall = jnp.where((at // 128 == high[:, None]) & inside, code, 0).astype(jnp.bfloat16)
    wide = (at[:, None] % 128 == jnp.arange(128, dtype=jnp.int32)).astype(jnp.bfloat16)
    return jnp.dot(tall, wide, preferred_element_type=jnp.float32).reshape(-1)[:capacity]


def on_device(tokens, cotangent, seq_group, block_slot, master, first_moment, second_moment):
    tensor_count = lax.axis_size("tensor")
    tensor_rank = lax.axis_index("tensor")
    owner_index = lax.axis_index("dp")
    owner_count = lax.axis_size("dp")
    local_rows, d = tokens.shape
    width_local = d // tensor_count
    heads_local = HEADS // tensor_count
    inner = heads_local * HD
    ff = FF // tensor_count
    seq_count = seq_group.shape[0]
    rows = local_rows * tensor_count
    seq_len = rows // seq_count
    capacity, block_width = master.shape[1:]
    block_count = block_slot.shape[0]

    span = -(-capacity // 16) * 16
    table_rows = owner_count * span
    slots = block_slot // capacity * span + block_slot % capacity
    side, core_index = tensor_rank // 2, tensor_rank % 2
    core = core_index.astype(jnp.int32).reshape(1)
    ends = (d * 3 * inner, d * 3 * inner + inner * d, d * 3 * inner + inner * d + d * ff, d * 3 * inner + inner * d + 2 * d * ff)
    own_slots = jnp.pad(master[0].astype(jnp.bfloat16), ((0, span - capacity), (0, 0)))
    slot_arrays, slot_starts = collect_slots(own_slots, owner_index, owner_count, span)
    far_x, far_back = (lax.ppermute(a, "tensor", FAR) for a in (tokens, cotangent))
    near_x, near_back = (lax.ppermute(a, "tensor", NEAR) for a in (tokens, cotangent))
    classes = slot_classes(block_slot, owner_index * capacity, capacity, tuple(e // block_width for e in ends))
    far_x, far_back, near_x, near_back, slot_arrays, slots, classes = lax.optimization_barrier(
        (far_x, far_back, near_x, near_back, slot_arrays, slots, classes)
    )
    both_x, both_back = (lax.ppermute(a, "tensor", NEAR) for a in (far_x, far_back))
    x_parts = (tokens, near_x, far_x, both_x)
    back_parts = (cotangent, near_back, far_back, both_back)
    w_qkv, w_o, w_up, w_dn, own_norms = unpack(slot_arrays, slot_starts, slots, table_rows, d, inner, ff)
    norm_rows_all = lax.all_gather(own_norms.reshape(1, 4, width_local), "tensor", axis=0, tiled=True)
    norms = jnp.transpose(norm_rows_all, (1, 0, 2)).reshape(4, d).astype(jnp.float32)
    tables = turn_tables(seq_len)

    q, k, v, d_out, hidden, second_stay, second_give, grad_down, grad_up, stat_two, squares_two = dense(
        core, x_parts, back_parts, w_qkv, w_o, w_up, w_dn, norms, tables, seq_count, 256
    )
    mixed, dq, dk, dv = attend(q, k, v, d_out, tables, seq_count, 512, heads_local)
    first_stay, first_give, grad_qkv, grad_o, stat_one, squares_one = grads(
        core, x_parts, back_parts, mixed, dq, dk, dv, w_qkv, norms, seq_count, 256
    )
    second_kept, second_sent = meet(second_stay, second_give)
    first_kept, first_sent = meet(first_stay, first_give)

    in_order = lambda pair: jnp.where(side == 0, pair, pair[::-1])
    squares = jnp.sum(squares_one + squares_two, axis=1)
    squares = jnp.concatenate([squares[:1], in_order(squares[1:])])
    stats = in_order(jnp.concatenate([stat_one, stat_two], axis=1))
    summed = lax.psum(jnp.concatenate([stats.reshape(-1), squares]), "tensor")
    stats = summed[:-3].reshape(seq_count, 4, d)
    squares = summed[-3:]
    both = squares[0] + jnp.sum((stats[0] + stats[1]) ** 2)
    each = squares[1:] + jnp.sum(stats * stats, axis=(1, 2))
    groups = jnp.arange(seq_count, dtype=jnp.int32)
    held = (seq_group[None, :] == groups[:, None]).astype(jnp.float32)
    sole = held[:, 0] * each[0] + held[:, 1] * each[1]
    group_norms = jnp.sqrt(jnp.where(held[:, 0] * held[:, 1] > 0, both, sole))
    clip = 1.0 / jnp.maximum(group_norms, 1.0)
    c = jnp.where(seq_group == 0, clip[0], clip[1])
    own_stats = lax.dynamic_slice_in_dim(stats, tensor_rank * width_local, width_local, 2)
    own_stats = (c[0] * own_stats[0] + c[1] * own_stats[1]).reshape(-1, block_width)
    local_clip = in_order(c)
    local_clip, second_sent, first_sent = lax.optimization_barrier((local_clip, second_sent, first_sent))
    second_sum, first_sum = close(second_kept, second_sent), close(first_kept, first_sent)
    spans, pack_at = pack_starts(owner_index, owner_count, span)
    packed = pack(
        grad_qkv, grad_o, grad_up, grad_down, own_stats, local_clip, slots, pack_at, spans, table_rows, d, inner, ff
    )
    branch_stay, branch_give = branch_of(core, mixed, hidden, w_o, w_dn, 512)
    branch_sum = close(*meet(branch_stay, branch_give))
    owned = sum_to_owners(packed, owner_index, owner_count)[:capacity].astype(jnp.float32)

    classes = classes[:, None]
    learn_rate = jnp.where(
        classes == 2, (seq_len / (5.0 * d)) ** 0.5, jnp.where(classes == 3, FF ** (-0.5), jnp.where(classes == 4, 0.1, d ** (-0.5)))
    )
    weight_decay = jnp.where(classes == 4, 0.0, 0.1)
    owned = jnp.where(classes > 0, owned, 0.0)
    old = master[0]
    new_one = beta_one * first_moment[0] + (1.0 - beta_one) * owned
    new_two = beta_two * second_moment[0] + (1.0 - beta_two) * owned * owned
    new_weight = old - learn_rate * (new_one / (jnp.sqrt(new_two) + eps_adam) + weight_decay * old)
    flat = lax.optimization_barrier(tuple(a.reshape(-1) for a in (new_weight, new_one, new_two)))
    new_weight, new_one, new_two = (a.reshape(master.shape) for a in flat)

    output = (tokens.astype(jnp.float32) + branch_sum).astype(jnp.bfloat16)
    own = tokens.astype(jnp.float32)
    centred = own - jnp.mean(own, axis=-1, keepdims=True)
    inverse = lax.rsqrt(jnp.mean(centred * centred, axis=-1, keepdims=True) + eps_norm)
    xhat = centred * inverse
    grad_input = cotangent.astype(jnp.float32)
    for total, gain in ((first_sum, norms[0]), (second_sum, norms[2])):
        scaled = total * gain
        mean = jnp.mean(scaled, axis=1, keepdims=True)
        cross = jnp.mean(scaled * xhat, axis=1, keepdims=True)
        grad_input = grad_input + inverse * (scaled - mean - xhat * cross)
    return (output, grad_input, group_norms, new_weight, new_one, new_two)


def solution(mesh):
    rows = P(("dp", "tensor"), None)
    slots = P("tensor", "dp", None)
    return jax.shard_map(
        on_device,
        mesh=mesh,
        in_specs=(rows, rows, P("dp"), P(), slots, slots, slots),
        out_specs=(rows, rows, P("dp"), slots, slots, slots),
        check_vma=False,
    )
```

```python
import functools
import jax
import jax.numpy as jnp
from jax import lax
from jax.experimental import pallas as pl
from jax.experimental.pallas import tpu as pltpu
from jax.sharding import PartitionSpec as P

HEADS = 12
HD = 64
ROT = 16
FF = 3072

eps_norm = 1e-05
eps_adam = 1e-08
beta_one = 0.5
beta_two = 0.6
root_half = 0.7071067811865476
inv_root_tau = 0.3989422804014327
PART = 256
VMEM_BYTES = 60 * 1024 * 1024


def dot_nn(left, right):
    return lax.dot_general(
        left, right, (((1,), (0,)), ((), ())), preferred_element_type=jnp.float32
    )


def dot_nt(left, right):
    return lax.dot_general(
        left, right, (((1,), (1,)), ((), ())), preferred_element_type=jnp.float32
    )


def dot_tn(left, right):
    return lax.dot_general(
        left, right, (((0,), (0,)), ((), ())), preferred_element_type=jnp.float32
    )


def turn_tables(seq_len):
    half = ROT // 2
    frequency = 10000.0 ** (-2.0 * jnp.arange(half, dtype=jnp.float32) / ROT)
    angles = jnp.arange(seq_len, dtype=jnp.float32)[:, None] * frequency[None, :]
    cosine, sine = jnp.cos(angles), jnp.sin(angles)
    rest = HD - ROT
    ones = jnp.ones((seq_len, rest), jnp.float32)
    zeros = jnp.zeros((seq_len, rest), jnp.float32)
    blank = jnp.zeros((seq_len, half), jnp.float32)
    keep = jnp.concatenate([cosine, cosine, ones], axis=1)
    low = jnp.concatenate([sine, blank, zeros], axis=1)
    high = jnp.concatenate([blank, sine, zeros], axis=1)
    return tuple(jnp.tile(t, (1, 128 // HD)) for t in (keep, low, high))


def turn(rows, keep, low, high, sign):
    half = ROT // 2
    pieces = []
    for start in range(0, rows.shape[1], 128):
        piece = rows[:, start : start + 128]
        ahead = pltpu.roll(piece, 128 - half, 1)
        behind = pltpu.roll(piece, half, 1)
        pieces.append(piece * keep + sign * (behind * high - ahead * low))
    return jnp.concatenate(pieces, axis=1)


def norm_rows(rows):
    mean = jnp.mean(rows, axis=-1, keepdims=True)
    centred = rows - mean
    inverse = lax.rsqrt(jnp.mean(centred * centred, axis=-1, keepdims=True) + eps_norm)
    return centred * inverse


def pair_squares(first, second):
    both = first + second
    parts = [both * both, first * first, second * second]
    return jnp.concatenate([jnp.sum(p, axis=0, keepdims=True) for p in parts], axis=0)


def pick(place, own, near, far, both):
    low = jnp.where(place == 0, own[...], near[...])
    high = jnp.where(place == 2, far[...], both[...])
    return jnp.where(place < 2, low, high)


def put_pair(place, rows, stay_ref, give_ref):
    @pl.when(place % 2 == 0)
    def _():
        stay_ref[...] = rows

    @pl.when(place % 2 == 1)
    def _():
        give_ref[...] = rows


def piece_specs(tile, width, per_piece):
    def at(n):
        def index(step, core_ref):
            return (jnp.where(((step // per_piece) ^ core_ref[0]) == n, step % per_piece, 0), 0)

        return pl.BlockSpec((tile, width), index)

    return [at(n) for n in range(4)]


def pair_specs(tile, width, per_piece):
    def at(parity):
        def index(step, core_ref):
            piece = step // per_piece
            first = piece // 2 * per_piece
            idle = jnp.where(piece % 2 == 1, first + per_piece - 1, jnp.maximum(first - 1, 0))
            return (jnp.where((piece ^ core_ref[0]) % 2 == parity, first + step % per_piece, idle), 0)

        return pl.BlockSpec((tile, width), index)

    return [at(0), at(1)]


def dense_kernel(
    tiles_per_seq, core_ref, x0_ref, x1_ref, x2_ref, x3_ref, g0_ref, g1_ref, g2_ref, g3_ref,
    wqkv_ref, wo_ref, wup_ref, wdn_ref, nrm_ref, keep_ref, low_ref, high_ref,
    q_ref, k_ref, v_ref, do_ref, hb_ref, stay_ref, give_ref, gwd_ref, gwu_ref, gn_ref, sq_ref,
):
    step = pl.program_id(0)
    seq = step // tiles_per_seq
    place = (2 * step // tiles_per_seq) ^ core_ref[0]

    @pl.when(step == 0)
    def _():
        gwd_ref[...] = jnp.zeros_like(gwd_ref)
        gwu_ref[...] = jnp.zeros_like(gwu_ref)
        gn_ref[...] = jnp.zeros_like(gn_ref)

    xhat = norm_rows(pick(place, x0_ref, x1_ref, x2_ref, x3_ref).astype(jnp.float32))
    first_in = (xhat * nrm_ref[0:1, :] + nrm_ref[1:2, :]).astype(jnp.bfloat16)
    second_in = (xhat * nrm_ref[2:3, :] + nrm_ref[3:4, :]).astype(jnp.bfloat16)
    back = pick(place, g0_ref, g1_ref, g2_ref, g3_ref)
    hidden_pre = dot_nn(second_in, wup_ref[...])
    grad_hidden = dot_nt(back, wdn_ref[...])
    cumulative = 0.5 * (1.0 + lax.erf(hidden_pre * root_half))
    density = jnp.exp(-0.5 * hidden_pre * hidden_pre) * inv_root_tau
    hidden = (hidden_pre * cumulative).astype(jnp.bfloat16)
    hb_ref[...] = hidden
    grad_pre = (grad_hidden * (cumulative + hidden_pre * density)).astype(jnp.bfloat16)
    projected = dot_nn(first_in, wqkv_ref[...])
    keep, low, high = keep_ref[...], low_ref[...], high_ref[...]
    q_ref[...] = (turn(projected[:, :PART], keep, low, high, 1.0) * HD ** (-0.5)).astype(jnp.bfloat16)
    k_ref[...] = turn(projected[:, PART : 2 * PART], keep, low, high, 1.0).astype(jnp.bfloat16)
    v_ref[...] = projected[:, 2 * PART :].astype(jnp.bfloat16)
    do_ref[...] = dot_nt(back, wo_ref[...]).astype(jnp.bfloat16)
    gwd_ref[seq] += dot_tn(hidden, back)
    gwu_ref[seq] += dot_tn(second_in, grad_pre)
    second_back = dot_nt(grad_pre, wup_ref[...]).astype(jnp.bfloat16)
    put_pair(place, second_back, stay_ref, give_ref)
    second_back = second_back.astype(jnp.float32)
    gn_ref[seq] += jnp.concatenate(
        [
            jnp.sum(second_back * xhat, axis=0, keepdims=True),
            jnp.sum(second_back, axis=0, keepdims=True),
        ],
        axis=0,
    )

    @pl.when(step == pl.num_programs(0) - 1)
    def _():
        sq_ref[...] = pair_squares(gwd_ref[0], gwd_ref[1]) + pair_squares(gwu_ref[0], gwu_ref[1])


def attend_kernel(
    block, heads, q_ref, k_ref, v_ref, do_ref, keep_ref, low_ref, high_ref,
    ao_ref, dq_ref, dk_ref, dv_ref, s_s, p_s, m_s, l_s, o_s, dk_s, dv_s, qh_s, doh_s, qt_s, dot_s,
):
    i = pl.program_id(1)
    last = pl.num_programs(1) - 1

    @pl.when(i == 0)
    def _():
        dk_s[...] = jnp.zeros_like(dk_s)
        dv_s[...] = jnp.zeros_like(dv_s)

    lane_head = lax.broadcasted_iota(jnp.int32, (block, PART), 1) // HD
    qt_s[...] = q_ref[...].T
    zero = jnp.zeros((), jnp.bfloat16)
    row = lax.broadcasted_iota(jnp.int32, (block, block), 0)
    col = lax.broadcasted_iota(jnp.int32, (block, block), 1)
    each = range(heads)
    dims = [slice(h * HD, (h + 1) * HD) for h in each]

    def rows_of(j):
        return pl.ds(pl.multiple_of(j * block, block), block)

    def fold(op, wide):
        folded = wide[:, :128]
        for c in range(128, block, 128):
            folded = op(folded, wide[:, c : c + 128])
        return folded

    def pick_heads(parts):
        rows = parts[0]
        for h in each[1:]:
            rows = jnp.where(lane_head == h, parts[h], rows)
        return jnp.where(lane_head < heads, rows, 0.0)

    for h in each:
        qh_s[h] = jnp.where(lane_head == h, q_ref[...], zero)
        scores = dot_nt(qh_s[h], k_ref[rows_of(i), :])
        scores = jnp.where(row >= col, scores, -1e30)
        s_s[i, h] = scores
        m_s[h] = fold(jnp.maximum, scores)

    def score(j, _):
        for h in each:
            scores = dot_nt(qh_s[h], k_ref[rows_of(j), :])
            s_s[j, h] = scores
            m_s[h] = jnp.maximum(m_s[h], fold(jnp.maximum, scores))
        return 0

    lax.fori_loop(0, i, score, 0)
    for h in each:
        m_s[h] = jnp.broadcast_to(jnp.max(m_s[h], axis=1, keepdims=True), m_s.shape[1:])
    l_s[...] = jnp.zeros_like(l_s)
    o_s[...] = jnp.zeros_like(o_s)

    def ahead(j, _):
        for h in each:
            probs = jnp.exp(s_s[j, h] - m_s[h][:, :1])
            l_s[h] += fold(jnp.add, probs)
            probs = probs.astype(jnp.bfloat16)
            p_s[j, h] = probs
            o_s[h] += dot_nn(probs, v_ref[rows_of(j), :])
        return 0

    lax.fori_loop(0, i + 1, ahead, 0)
    outs = []
    for h in each:
        inverse = 1.0 / jnp.sum(l_s[h], axis=1, keepdims=True)
        out = o_s[h] * inverse
        do_head = jnp.where(lane_head == h, do_ref[...], zero).astype(jnp.float32)
        delta = jnp.sum(do_head * out, axis=1, keepdims=True)
        outs.append(out)
        scaled = (do_head * inverse).astype(jnp.bfloat16)
        doh_s[h] = scaled
        dot_s[dims[h], :] = scaled.T[dims[h], :]
        l_s[h] = jnp.broadcast_to(delta * inverse, l_s.shape[1:])
    ao_ref[...] = pick_heads(outs).astype(jnp.bfloat16)
    o_s[...] = jnp.zeros_like(o_s)

    def behind(j, _):
        for h in each:
            grad_probs = dot_nt(doh_s[h], v_ref[rows_of(j), :])
            probs = p_s[j, h]
            shifted = grad_probs - l_s[h][:, :1]
            grad_scores = (probs.astype(jnp.float32) * shifted).astype(jnp.bfloat16)
            o_s[h] += dot_nn(grad_scores, k_ref[rows_of(j), :])
            dk_s[dims[h], rows_of(j)] += dot_nn(qt_s[dims[h], :], grad_scores)
            dv_s[dims[h], rows_of(j)] += dot_nn(dot_s[dims[h], :], probs)
        return 0

    lax.fori_loop(0, i + 1, behind, 0)
    here = rows_of(i)
    grad_q = pick_heads([o_s[h] for h in each])
    dq_ref[...] = (
        turn(grad_q, keep_ref[here, :], low_ref[here, :], high_ref[here, :], -1.0) * HD ** (-0.5)
    ).astype(jnp.bfloat16)

    @pl.when(i == last)
    def _():
        dk_ref[...] = turn(dk_s[...].T, keep_ref[...], low_ref[...], high_ref[...], -1.0).astype(jnp.bfloat16)
        dv_ref[...] = dv_s[...].T.astype(jnp.bfloat16)


def grads_kernel(
    tiles_per_seq, core_ref, x0_ref, x1_ref, x2_ref, x3_ref, g0_ref, g1_ref, g2_ref, g3_ref,
    ao_ref, dq_ref, dk_ref, dv_ref, wqkv_ref, nrm_ref,
    stay_ref, give_ref, gwq_ref, gwo_ref, gn_ref, sq_ref,
):
    step = pl.program_id(0)
    seq = step // tiles_per_seq
    place = (2 * step // tiles_per_seq) ^ core_ref[0]

    @pl.when(step == 0)
    def _():
        gwq_ref[...] = jnp.zeros_like(gwq_ref)
        gwo_ref[...] = jnp.zeros_like(gwo_ref)
        gn_ref[...] = jnp.zeros_like(gn_ref)

    xhat = norm_rows(pick(place, x0_ref, x1_ref, x2_ref, x3_ref).astype(jnp.float32))
    first_in = (xhat * nrm_ref[0:1, :] + nrm_ref[1:2, :]).astype(jnp.bfloat16)
    grad_qkv = jnp.concatenate([dq_ref[...], dk_ref[...], dv_ref[...]], axis=1)
    first_back = dot_nt(grad_qkv, wqkv_ref[...]).astype(jnp.bfloat16)
    put_pair(place, first_back, stay_ref, give_ref)
    gwq_ref[seq] += dot_tn(first_in, grad_qkv)
    gwo_ref[seq] += dot_tn(ao_ref[...], pick(place, g0_ref, g1_ref, g2_ref, g3_ref))
    first_back = first_back.astype(jnp.float32)
    gn_ref[seq] += jnp.concatenate(
        [
            jnp.sum(first_back * xhat, axis=0, keepdims=True),
            jnp.sum(first_back, axis=0, keepdims=True),
        ],
        axis=0,
    )

    @pl.when(step == pl.num_programs(0) - 1)
    def _():
        sq_ref[...] = pair_squares(gwq_ref[0], gwq_ref[1]) + pair_squares(gwo_ref[0], gwo_ref[1])


def branch_kernel(per_piece, core_ref, ao_ref, hb_ref, wo_ref, wdn_ref, stay_ref, give_ref):
    place = (pl.program_id(0) // per_piece) ^ core_ref[0]
    rows = (dot_nn(ao_ref[...], wo_ref[...]) + dot_nn(hb_ref[...], wdn_ref[...])).astype(jnp.bfloat16)
    put_pair(place, rows, stay_ref, give_ref)


def whole(shape):
    return pl.BlockSpec(shape, lambda *_: (0,) * len(shape))


def params(dims):
    return pltpu.CompilerParams(
        dimension_semantics=("arbitrary",) * dims, vmem_limit_bytes=VMEM_BYTES
    )


def dense(core, x_parts, back_parts, w_qkv, w_o, w_up, w_dn, norms, tables, seq_count, tile):
    rows, d = 4 * x_parts[0].shape[0], x_parts[0].shape[1]
    steps = rows // tile
    per_seq = steps // seq_count
    row = lambda width: pl.BlockSpec((tile, width), lambda s, _: (s, 0))
    table = pl.BlockSpec((tile, 128), lambda s, _: (lax.rem(s, per_seq), 0))
    act = lambda width: jax.ShapeDtypeStruct((rows, width), jnp.bfloat16)
    pair = jax.ShapeDtypeStruct((rows // 2, d), jnp.bfloat16)
    ff = w_up.shape[1]
    grad = jax.ShapeDtypeStruct((seq_count, ff, d), jnp.float32)
    grad_up = jax.ShapeDtypeStruct((seq_count, d, ff), jnp.float32)
    stat = jax.ShapeDtypeStruct((seq_count, 2, d), jnp.float32)
    squares = jax.ShapeDtypeStruct((3, d), jnp.float32)
    pieces = piece_specs(tile, d, steps // 4)
    return pl.pallas_call(
        functools.partial(dense_kernel, per_seq),
        name="dense",
        grid_spec=pltpu.PrefetchScalarGridSpec(
            num_scalar_prefetch=1,
            grid=(steps,),
            in_specs=pieces + pieces + [whole(w_qkv.shape), whole(w_o.shape), whole(w_up.shape), whole(w_dn.shape),
                                        whole(norms.shape), table, table, table],
            out_specs=[row(PART), row(PART), row(PART), row(PART), row(ff)] + pair_specs(tile, d, steps // 4)
            + [whole(grad.shape), whole(grad_up.shape), whole(stat.shape), whole(squares.shape)],
        ),
        out_shape=[act(PART), act(PART), act(PART), act(PART), act(ff), pair, pair, grad, grad_up, stat, squares],
        compiler_params=params(1),
    )(core, *x_parts, *back_parts, w_qkv, w_o, w_up, w_dn, norms, *tables)


def attend(q, k, v, d_out, tables, seq_count, block, heads):
    rows = q.shape[0]
    seq_len = rows // seq_count
    blocks = seq_len // block
    part = pl.BlockSpec((block, PART), lambda s, i: (s * blocks + i, 0))
    full = pl.BlockSpec((seq_len, PART), lambda s, i: (s, 0))
    act = jax.ShapeDtypeStruct((rows, PART), jnp.bfloat16)
    table = whole((seq_len, 128))
    return pl.pallas_call(
        functools.partial(attend_kernel, block, heads),
        name="attend",
        grid=(seq_count, blocks),
        in_specs=[part, full, full, part, table, table, table],
        out_specs=[part, part, full, full],
        out_shape=[act] * 4,
        scratch_shapes=[
            pltpu.VMEM((blocks, heads, block, block), jnp.float32),
            pltpu.VMEM((blocks, heads, block, block), jnp.bfloat16),
            pltpu.VMEM((heads, block, 128), jnp.float32),
            pltpu.VMEM((heads, block, 128), jnp.float32),
            pltpu.VMEM((heads, block, PART), jnp.float32),
            pltpu.VMEM((PART, seq_len), jnp.float32),
            pltpu.VMEM((PART, seq_len), jnp.float32),
            pltpu.VMEM((heads, block, PART), jnp.bfloat16),
            pltpu.VMEM((heads, block, PART), jnp.bfloat16),
            pltpu.VMEM((PART, block), jnp.bfloat16),
            pltpu.VMEM((PART, block), jnp.bfloat16),
        ],
        compiler_params=params(2),
    )(q, k, v, d_out, *tables)


def grads(core, x_parts, back_parts, ao, dq, dk, dv, w_qkv, norms, seq_count, tile):
    rows, d = 4 * x_parts[0].shape[0], x_parts[0].shape[1]
    steps = rows // tile
    per_seq = steps // seq_count
    row = lambda width: pl.BlockSpec((tile, width), lambda s, _: (s, 0))
    pair = jax.ShapeDtypeStruct((rows // 2, d), jnp.bfloat16)
    grad_q = jax.ShapeDtypeStruct((seq_count, d, 3 * PART), jnp.float32)
    grad_o = jax.ShapeDtypeStruct((seq_count, PART, d), jnp.float32)
    stat = jax.ShapeDtypeStruct((seq_count, 2, d), jnp.float32)
    squares = jax.ShapeDtypeStruct((3, d), jnp.float32)
    pieces = piece_specs(tile, d, steps // 4)
    return pl.pallas_call(
        functools.partial(grads_kernel, per_seq),
        name="grads",
        grid_spec=pltpu.PrefetchScalarGridSpec(
            num_scalar_prefetch=1,
            grid=(steps,),
            in_specs=pieces + pieces + [row(PART)] * 4 + [whole(w_qkv.shape), whole(norms.shape)],
            out_specs=pair_specs(tile, d, steps // 4)
            + [whole(grad_q.shape), whole(grad_o.shape), whole(stat.shape), whole(squares.shape)],
        ),
        out_shape=[pair, pair, grad_q, grad_o, stat, squares],
        compiler_params=params(1),
    )(core, *x_parts, *back_parts, ao, dq, dk, dv, w_qkv, norms)


def branch_of(core, ao, hb, w_o, w_dn, tile):
    rows = ao.shape[0]
    d = w_o.shape[1]
    row = lambda width: pl.BlockSpec((tile, width), lambda s, _: (s, 0))
    pair = jax.ShapeDtypeStruct((rows // 2, d), jnp.bfloat16)
    return pl.pallas_call(
        functools.partial(branch_kernel, rows // tile // 4),
        name="branch",
        grid_spec=pltpu.PrefetchScalarGridSpec(
            num_scalar_prefetch=1,
            grid=(rows // tile,),
            in_specs=[row(ao.shape[1]), row(hb.shape[1]), whole(w_o.shape), whole(w_dn.shape)],
            out_specs=pair_specs(tile, d, rows // tile // 4),
        ),
        out_shape=[pair, pair],
        compiler_params=params(1),
    )(core, ao, hb, w_o, w_dn)


def swap_halves(piece):
    return pltpu.roll(piece, 64, 1)


def unpack_kernel(spans, counts, starts_ref, slots_ref, *refs):
    arrays = refs[: len(spans)]
    wqkv_ref, wo_ref, wup_ref, wdn_ref, nrm_ref, table_s, flat_s, wide_s = refs[len(spans) :]
    d, inner, ff = counts
    for n, (array, span) in enumerate(zip(arrays, spans)):
        start = starts_ref[n]

        @pl.when(start >= 0)
        def _():
            table_s[pl.ds(pl.multiple_of(start, 16), span), :] = array[...].astype(jnp.float32)

    blocks = slots_ref.shape[0]
    wide = 16

    def fetch(n, _):
        for u in range(wide):
            b = n * wide + u
            flat_s[pl.ds(b, 1), :] = table_s[pl.ds(slots_ref[b], 1), :]
        return 0

    lax.fori_loop(0, blocks // wide, fetch, 0)
    for b in range(blocks // wide * wide, blocks):
        flat_s[pl.ds(b, 1), :] = table_s[pl.ds(slots_ref[b], 1), :]

    half = lax.broadcasted_iota(jnp.int32, (d // 2, 128), 1) < 64
    e = [flat_s[pl.ds(c, d // 2, stride=9), :] for c in range(9)]
    even = [
        e[0], jnp.where(half, e[1], 0.0),
        jnp.where(half, swap_halves(e[1]), swap_halves(e[2])), jnp.where(half, swap_halves(e[2]), 0.0),
        e[3], jnp.where(half, e[4], 0.0),
    ]
    odd = [
        jnp.where(half, swap_halves(e[4]), swap_halves(e[5])), jnp.where(half, swap_halves(e[5]), 0.0),
        e[6], jnp.where(half, e[7], 0.0),
        jnp.where(half, swap_halves(e[7]), swap_halves(e[8])), jnp.where(half, swap_halves(e[8]), 0.0),
    ]
    for c in range(6):
        wide_s[pl.ds(0, d // 2, stride=2), :] = even[c]
        wide_s[pl.ds(1, d // 2, stride=2), :] = odd[c]
        wqkv_ref[:, c * 128 : (c + 1) * 128] = wide_s[...].astype(jnp.bfloat16)
    base = d * 3 * inner // 128
    step = d // 128
    for ref, height in ((wo_ref, inner), (wup_ref, d), (wdn_ref, ff)):
        for c in range(step):
            ref[:height, c * 128 : (c + 1) * 128] = flat_s[pl.ds(base + c, height, stride=step), :].astype(jnp.bfloat16)
        base += height * step
    wo_ref[inner:, :] = jnp.zeros_like(wo_ref[inner:, :])
    nrm_ref[...] = flat_s[pl.ds(base, blocks - base), :].astype(jnp.bfloat16)


def unpack(arrays, starts, slots, table_rows, d, inner, ff):
    spans = tuple(a.shape[0] for a in arrays)
    blocks = slots.shape[0]
    smem = pl.BlockSpec(memory_space=pltpu.SMEM)
    vmem = pl.BlockSpec(memory_space=pltpu.VMEM)
    end = (d * 3 * inner + inner * d + 2 * d * ff) // 128
    weight = lambda h, w: jax.ShapeDtypeStruct((h, w), jnp.bfloat16)
    return pl.pallas_call(
        functools.partial(unpack_kernel, spans, (d, inner, ff)),
        name="unpack",
        in_specs=[smem, smem] + [vmem] * len(arrays),
        out_specs=[vmem] * 5,
        out_shape=[weight(d, 3 * PART), weight(PART, d), weight(d, ff), weight(ff, d), weight(blocks - end, 128)],
        scratch_shapes=[
            pltpu.VMEM((table_rows, 128), jnp.float32),
            pltpu.VMEM((-(-blocks // 16) * 16, 128), jnp.float32),
            pltpu.VMEM((d, 128), jnp.float32),
        ],
        compiler_params=pltpu.CompilerParams(vmem_limit_bytes=VMEM_BYTES),
    )(starts, slots, *arrays)


def pack_kernel(spans, counts, starts_ref, slots_ref, clip_ref, gwq_ref, gwo_ref, gwu_ref, gwd_ref, stat_ref, *refs):
    outs = refs[: len(spans)]
    flat_s, slot_s, wide_s = refs[len(spans) :]
    d, inner, ff = counts
    one, two = clip_ref[0], clip_ref[1]
    half = lax.broadcasted_iota(jnp.int32, (d // 2, 128), 1) < 64
    even, odd = [], []
    for c in range(6):
        cols = slice(c * 128, (c + 1) * 128)
        wide_s[c] = gwq_ref[0, :, cols] * one + gwq_ref[1, :, cols] * two
        even.append(wide_s[c, pl.ds(0, d // 2, stride=2), :])
        odd.append(wide_s[c, pl.ds(1, d // 2, stride=2), :])
    q0, q1, k0, k1, v0, v1 = even
    r0, r1, s0, s1, u0, u1 = odd
    pieces = [
        q0, jnp.where(half, q1, swap_halves(k0)), jnp.where(half, swap_halves(k0), swap_halves(k1)),
        v0, jnp.where(half, v1, swap_halves(r0)), jnp.where(half, swap_halves(r0), swap_halves(r1)),
        s0, jnp.where(half, s1, swap_halves(u0)), jnp.where(half, swap_halves(u0), swap_halves(u1)),
    ]
    for c in range(9):
        flat_s[pl.ds(c, d // 2, stride=9), :] = pieces[c]
    base = d * 3 * inner // 128
    step = d // 128
    for ref, height in ((gwo_ref, inner), (gwu_ref, d), (gwd_ref, ff)):
        for c in range(step):
            cols = slice(c * 128, (c + 1) * 128)
            flat_s[pl.ds(base + c, height, stride=step), :] = ref[0, :height, cols] * one + ref[1, :height, cols] * two
        base += height * step
    blocks = slots_ref.shape[0]
    flat_s[pl.ds(base, blocks - base), :] = stat_ref[...]
    wide = 16

    def place(n, _):
        for u in range(wide):
            b = n * wide + u
            slot_s[pl.ds(slots_ref[b], 1), :] = flat_s[pl.ds(b, 1), :]
        return 0

    lax.fori_loop(0, blocks // wide, place, 0)
    for b in range(blocks // wide * wide, blocks):
        slot_s[pl.ds(slots_ref[b], 1), :] = flat_s[pl.ds(b, 1), :]
    for n, (out, span) in enumerate(zip(outs, spans)):
        out[...] = slot_s[pl.ds(pl.multiple_of(starts_ref[n], 16), span), :].astype(jnp.bfloat16)


def pack(grad_qkv, grad_o, grad_up, grad_down, stat, clip, slots, starts, spans, table_rows, d, inner, ff):
    blocks = slots.shape[0]
    smem = pl.BlockSpec(memory_space=pltpu.SMEM)
    vmem = pl.BlockSpec(memory_space=pltpu.VMEM)
    return pl.pallas_call(
        functools.partial(pack_kernel, spans, (d, inner, ff)),
        name="pack",
        in_specs=[smem] * 3 + [vmem] * 5,
        out_specs=[vmem] * len(spans),
        out_shape=[jax.ShapeDtypeStruct((s, 128), jnp.bfloat16) for s in spans],
        scratch_shapes=[
            pltpu.VMEM((-(-blocks // 16) * 16, 128), jnp.float32),
            pltpu.VMEM((table_rows, 128), jnp.float32),
            pltpu.VMEM((6, d, 128), jnp.float32),
        ],
        compiler_params=pltpu.CompilerParams(vmem_limit_bytes=VMEM_BYTES),
    )(starts, slots, clip, grad_qkv, grad_o, grad_up, grad_down, stat)


def ladder(step, test, outer):
    return [
        (2 * z + x, 2 * (z + step) + x) for z in range(outer) for x in range(2) if test(z) and 0 <= z + step < outer
    ]


def cross(test, outer):
    return [(2 * z + x, 2 * z + 1 - x) for z in range(outer) for x in range(2) if test(z)]


def collect_slots(own, owner_index, owner_count, span):
    if owner_count != 8:
        return [lax.all_gather(own, "dp", axis=0, tiled=True)], jnp.zeros((1,), jnp.int32)
    z, x = owner_index // 2, owner_index % 2
    arrays = [own, lax.ppermute(own, "dp", cross(lambda q: True, 4))]
    owners = [2 * z + x, 2 * z + 1 - x]
    up = down = own
    for hop in range(3):
        up = lax.ppermute(up, "dp", ladder(1, lambda q: q >= hop, 4))
        down = lax.ppermute(down, "dp", ladder(-1, lambda q: q <= 3 - hop, 4))
        up_x = lax.ppermute(up, "dp", cross(lambda q: q > hop, 4))
        down_x = lax.ppermute(down, "dp", cross(lambda q: q < 3 - hop, 4))
        arrays += [up, down, up_x, down_x]
        low, high = z - 1 - hop, z + 1 + hop
        for there, has in ((low, low >= 0), (high, high < 4)):
            owners.append(jnp.where(has, 2 * there + x, -1))
        for there, has in ((low, low >= 0), (high, high < 4)):
            owners.append(jnp.where(has, 2 * there + 1 - x, -1))
    owners = jnp.stack(owners)
    return arrays, jnp.where(owners >= 0, owners * span, -1).astype(jnp.int32)


def pack_starts(owner_index, owner_count, span):
    if owner_count != 8:
        return (owner_count * span,), jnp.zeros((1,), jnp.int32)
    z, x = owner_index // 2, owner_index % 2
    order = jnp.array([[3, 2, 1, 0], [3, 0, 2, 1], [0, 3, 1, 2], [0, 1, 2, 3]], jnp.int32)[z]
    return (span,) * 8, jnp.concatenate([2 * order + 1 - x, 2 * order + x]).astype(jnp.int32) * span


def sum_to_owners(packed, owner_index, owner_count):
    if owner_count != 8:
        return lax.psum_scatter(packed[0], "dp", scatter_dimension=0, tiled=True)
    z = owner_index // 2
    part = [mine + lax.ppermute(give, "dp", cross(lambda q: True, 4)) for give, mine in zip(packed[:4], packed[4:])]
    up = lax.ppermute(part[0], "dp", ladder(1, lambda q: q == 0, 4))
    down = lax.ppermute(part[0], "dp", ladder(-1, lambda q: q == 3, 4))
    middle = jnp.where((z == 0) | (z == 3), part[1], part[0])
    up = lax.ppermute(middle + up, "dp", ladder(1, lambda q: q <= 1, 4))
    down = lax.ppermute(middle + down, "dp", ladder(-1, lambda q: q >= 2, 4))
    up = lax.ppermute(jnp.where(z == 2, part[1], part[2]) + up, "dp", ladder(1, lambda q: q <= 2, 4))
    down = lax.ppermute(jnp.where(z == 1, part[1], part[2]) + down, "dp", ladder(-1, lambda q: q >= 1, 4))
    return part[3] + up + down


NEAR = [(i, i ^ 1) for i in range(4)]
FAR = [(i, i ^ 2) for i in range(4)]


def meet(stay, give):
    got = lax.ppermute(give, "tensor", NEAR)
    both = stay.astype(jnp.float32) + got.astype(jnp.float32)
    rows = stay.shape[0] // 2
    return both[:rows], both[rows:].astype(jnp.bfloat16)


def close(kept, sent):
    return kept + lax.ppermute(sent, "tensor", FAR).astype(jnp.float32)


def slot_classes(slots, first, capacity, ends):
    block = jnp.arange(slots.shape[0], dtype=jnp.int32)
    code = jnp.where(block < ends[0], 1, jnp.where(block < ends[1], 2, jnp.where(block < ends[2], 1, jnp.where(block < ends[3], 3, 4))))
    at = slots - first
    high = jnp.arange(-(-capacity // 128), dtype=jnp.int32)
    inside = (at >= 0) & (at < capacity)
    tall = jnp.where((at // 128 == high[:, None]) & inside, code, 0).astype(jnp.bfloat16)
    wide = (at[:, None] % 128 == jnp.arange(128, dtype=jnp.int32)).astype(jnp.bfloat16)
    return jnp.dot(tall, wide, preferred_element_type=jnp.float32).reshape(-1)[:capacity]


def on_device(tokens, cotangent, seq_group, block_slot, master, first_moment, second_moment):
    tensor_count = lax.axis_size("tensor")
    tensor_rank = lax.axis_index("tensor")
    owner_index = lax.axis_index("dp")
    owner_count = lax.axis_size("dp")
    local_rows, d = tokens.shape
    width_local = d // tensor_count
    heads_local = HEADS // tensor_count
    inner = heads_local * HD
    ff = FF // tensor_count
    seq_count = seq_group.shape[0]
    rows = local_rows * tensor_count
    seq_len = rows // seq_count
    capacity, block_width = master.shape[1:]
    block_count = block_slot.shape[0]

    span = -(-capacity // 16) * 16
    table_rows = owner_count * span
    slots = block_slot // capacity * span + block_slot % capacity
    side, core_index = tensor_rank // 2, tensor_rank % 2
    core = core_index.astype(jnp.int32).reshape(1)
    ends = (d * 3 * inner, d * 3 * inner + inner * d, d * 3 * inner + inner * d + d * ff, d * 3 * inner + inner * d + 2 * d * ff)
    own_slots = jnp.pad(master[0].astype(jnp.bfloat16), ((0, span - capacity), (0, 0)))
    slot_arrays, slot_starts = collect_slots(own_slots, owner_index, owner_count, span)
    far_x, far_back = (lax.ppermute(a, "tensor", FAR) for a in (tokens, cotangent))
    near_x, near_back = (lax.ppermute(a, "tensor", NEAR) for a in (tokens, cotangent))
    classes = slot_classes(block_slot, owner_index * capacity, capacity, tuple(e // block_width for e in ends))
    near_x, near_back, slot_arrays, slots, classes = lax.optimization_barrier(
        (near_x, near_back, slot_arrays, slots, classes)
    )
    w_qkv, w_o, w_up, w_dn, own_norms = unpack(slot_arrays, slot_starts, slots, table_rows, d, inner, ff)
    far_x, far_back, own_norms = lax.optimization_barrier((far_x, far_back, own_norms))
    both_x, both_back = (lax.ppermute(a, "tensor", NEAR) for a in (far_x, far_back))
    x_parts = (tokens, near_x, far_x, both_x)
    back_parts = (cotangent, near_back, far_back, both_back)
    norm_rows_all = lax.all_gather(own_norms.reshape(1, 4, width_local), "tensor", axis=0, tiled=True)
    norms = jnp.transpose(norm_rows_all, (1, 0, 2)).reshape(4, d).astype(jnp.float32)
    tables = turn_tables(seq_len)

    q, k, v, d_out, hidden, second_stay, second_give, grad_down, grad_up, stat_two, squares_two = dense(
        core, x_parts, back_parts, w_qkv, w_o, w_up, w_dn, norms, tables, seq_count, 256
    )
    mixed, dq, dk, dv = attend(q, k, v, d_out, tables, seq_count, 512, heads_local)
    first_stay, first_give, grad_qkv, grad_o, stat_one, squares_one = grads(
        core, x_parts, back_parts, mixed, dq, dk, dv, w_qkv, norms, seq_count, 256
    )
    second_kept, second_sent = meet(second_stay, second_give)
    first_kept, first_sent = meet(first_stay, first_give)

    in_order = lambda pair: jnp.where(side == 0, pair, pair[::-1])
    squares = jnp.sum(squares_one + squares_two, axis=1)
    squares = jnp.concatenate([squares[:1], in_order(squares[1:])])
    stats = in_order(jnp.concatenate([stat_one, stat_two], axis=1))
    summed = lax.psum(jnp.concatenate([stats.reshape(-1), squares]), "tensor")
    stats = summed[:-3].reshape(seq_count, 4, d)
    squares = summed[-3:]
    both = squares[0] + jnp.sum((stats[0] + stats[1]) ** 2)
    each = squares[1:] + jnp.sum(stats * stats, axis=(1, 2))
    groups = jnp.arange(seq_count, dtype=jnp.int32)
    held = (seq_group[None, :] == groups[:, None]).astype(jnp.float32)
    sole = held[:, 0] * each[0] + held[:, 1] * each[1]
    group_norms = jnp.sqrt(jnp.where(held[:, 0] * held[:, 1] > 0, both, sole))
    clip = 1.0 / jnp.maximum(group_norms, 1.0)
    c = jnp.where(seq_group == 0, clip[0], clip[1])
    own_stats = lax.dynamic_slice_in_dim(stats, tensor_rank * width_local, width_local, 2)
    own_stats = (c[0] * own_stats[0] + c[1] * own_stats[1]).reshape(-1, block_width)
    local_clip = in_order(c)
    local_clip, second_sent, first_sent = lax.optimization_barrier((local_clip, second_sent, first_sent))
    second_sum, first_sum = close(second_kept, second_sent), close(first_kept, first_sent)
    spans, pack_at = pack_starts(owner_index, owner_count, span)
    packed = pack(
        grad_qkv, grad_o, grad_up, grad_down, own_stats, local_clip, slots, pack_at, spans, table_rows, d, inner, ff
    )
    branch_stay, branch_give = branch_of(core, mixed, hidden, w_o, w_dn, 512)
    branch_sum = close(*meet(branch_stay, branch_give))
    owned = sum_to_owners(packed, owner_index, owner_count)[:capacity].astype(jnp.float32)

    classes = classes[:, None]
    learn_rate = jnp.where(
        classes == 2, (seq_len / (5.0 * d)) ** 0.5, jnp.where(classes == 3, FF ** (-0.5), jnp.where(classes == 4, 0.1, d ** (-0.5)))
    )
    weight_decay = jnp.where(classes == 4, 0.0, 0.1)
    owned = jnp.where(classes > 0, owned, 0.0)
    old = master[0]
    new_one = beta_one * first_moment[0] + (1.0 - beta_one) * owned
    new_two = beta_two * second_moment[0] + (1.0 - beta_two) * owned * owned
    new_weight = old - learn_rate * (new_one / (jnp.sqrt(new_two) + eps_adam) + weight_decay * old)
    flat = lax.optimization_barrier(tuple(a.reshape(-1) for a in (new_weight, new_one, new_two)))
    new_weight, new_one, new_two = (a.reshape(master.shape) for a in flat)

    output = (tokens.astype(jnp.float32) + branch_sum).astype(jnp.bfloat16)
    own = tokens.astype(jnp.float32)
    centred = own - jnp.mean(own, axis=-1, keepdims=True)
    inverse = lax.rsqrt(jnp.mean(centred * centred, axis=-1, keepdims=True) + eps_norm)
    xhat = centred * inverse
    grad_input = cotangent.astype(jnp.float32)
    for total, gain in ((first_sum, norms[0]), (second_sum, norms[2])):
        scaled = total * gain
        mean = jnp.mean(scaled, axis=1, keepdims=True)
        cross = jnp.mean(scaled * xhat, axis=1, keepdims=True)
        grad_input = grad_input + inverse * (scaled - mean - xhat * cross)
    return (output, grad_input, group_norms, new_weight, new_one, new_two)


def solution(mesh):
    rows = P(("dp", "tensor"), None)
    slots = P("tensor", "dp", None)
    return jax.shard_map(
        on_device,
        mesh=mesh,
        in_specs=(rows, rows, P("dp"), P(), slots, slots, slots),
        out_specs=(rows, rows, P("dp"), slots, slots, slots),
        check_vma=False,
    )
```
